512 devices in a mesh: seq: 32 (over x, z), head: 16 (over y, core).
Axes of the slice: x: 4, y: 8, z: 8, core: 2. Of those that a mesh axis runs over, the one named last changes fastest.
Arguments:
- queries: bfloat16 [32768, 2048], P('seq', 'head'), may hold values from -6 to 6
- key_rows: bfloat16 [32768, 2048], P('seq', 'head'), may hold values from -6 to 6
- value_rows: bfloat16 [32768, 4096], P('seq', 'head'), may hold values from -6 to 6
- out_gate: bfloat16 [32768, 4096], P('seq', 'head'), may hold values from -6 to 6
- write_rate: float32 [32, 32768], P('head', 'seq'), may hold values from 0.0009765625 to 1
- log_gate: float32 [32, 32768], P('head', 'seq'), may hold values from -1 to 0, as said below
- doc_start: int32 [32768], P('seq'), may hold values 0 or 1
- norm_gain: float32 [128], replicated, may hold values from 0.1 to 1.9
- out_weight: bfloat16 [4096, 2048], P('head'), may hold values from -0.125 to 0.125
Outputs:
- mixed: bfloat16 [32768, 2048], P('seq', 'head')
The draws below stay inside these ranges and needn't reach their ends.
Inputs may be any that keep to these rules, and one draw needn't show every extreme that they name: `log_gate`: log of the per-token decay factor of each value head's state.
All inputs are finite; a program needn't handle non-finite values. No bound on the sum of `doc_start` on one device may be relied on, other than what follows from the above.
Results may differ from the reference program's by a relative error of at most 0.027.
Values may be sent and summed in bfloat16 or wider, within the bound.
A program may use at most 128 MiB of HBM per device.

```python
import math
import jax
import jax.numpy as jnp
from jax import lax

D = 2048
VALUE_HEAD_COUNT = 32
HK = 16
DK = 128
DV = 128
SPAN = 64
TOK_DEV = 1024
SEQUENCE_TOKENS = 32768
N_HEAD = 16


def head_kinds(key):
    chooser = jax.random.uniform(jax.random.fold_in(key, 7), (VALUE_HEAD_COUNT, 1))
    fast_share = 0.35
    medium_share = 0.15
    fast_heads = chooser < fast_share
    medium_heads = (chooser >= fast_share) & (chooser < fast_share + medium_share)
    return (fast_heads, medium_heads)


def draw_write_rate(key, part):
    lanes = jax.random.split(jax.random.fold_in(key, 11), 2)
    fast_heads, medium_heads = head_kinds(key)
    strong_rates = jax.random.uniform(lanes[0], (VALUE_HEAD_COUNT, SEQUENCE_TOKENS), minval=0.05, maxval=1.0)
    lowest_rate = 0.25 * DK / SEQUENCE_TOKENS
    weak_rates = jnp.exp(jax.random.uniform(lanes[1], (VALUE_HEAD_COUNT, SEQUENCE_TOKENS), minval=math.log(lowest_rate), maxval=math.log(4.0 * lowest_rate)))
    chosen = jnp.where(fast_heads | medium_heads, strong_rates, weak_rates)
    return chosen.astype(jnp.float32)


def draw_log_gate(key, part):
    sequence_lanes = jax.random.split(jax.random.fold_in(key, 13), 7)
    fast_heads, medium_heads = head_kinds(key)
    fast_heads = fast_heads[:, :, None]
    slow_rate = jnp.exp(jax.random.uniform(sequence_lanes[1], (VALUE_HEAD_COUNT, 1, 1), minval=math.log(0.05 / SEQUENCE_TOKENS), maxval=math.log(1.0 / SEQUENCE_TOKENS)))
    fast_rate = jnp.exp(jax.random.uniform(sequence_lanes[2], (VALUE_HEAD_COUNT, 1, 1), minval=math.log(1.0 / 50.0), maxval=math.log(1.0 / 30.0)))
    base_rate = jnp.where(fast_heads, fast_rate, slow_rate)
    shard_factor = jnp.exp(jax.random.uniform(sequence_lanes[3], (VALUE_HEAD_COUNT, SEQUENCE_TOKENS // TOK_DEV, 1), minval=math.log(0.5), maxval=math.log(2.0)))
    token_factor = jnp.exp(jax.random.uniform(sequence_lanes[4], (VALUE_HEAD_COUNT, SEQUENCE_TOKENS // TOK_DEV, TOK_DEV), minval=math.log(0.5), maxval=math.log(2.0)))
    steady_decay_part = (base_rate * shard_factor * token_factor).reshape(VALUE_HEAD_COUNT, SEQUENCE_TOKENS)
    spike_token_index = jax.random.randint(sequence_lanes[5], (VALUE_HEAD_COUNT, 2, 1), 0, SEQUENCE_TOKENS)
    token_positions = jnp.arange(SEQUENCE_TOKENS, dtype=jnp.int32)
    spike_token_hits = jnp.any(token_positions[None, None, :] == spike_token_index, axis=1)
    spike_decay_keep = jax.random.uniform(sequence_lanes[6], (VALUE_HEAD_COUNT, SEQUENCE_TOKENS), minval=0.5, maxval=0.8)
    layer_output = -steady_decay_part + jnp.where(spike_token_hits, jnp.log(spike_decay_keep), 0.0)
    return layer_output.astype(jnp.float32)


def place_ends(values, key, low, top_value):
    longest = values.shape.index(max(values.shape))
    spots = []
    for shift in (0, 1):
        where = [jax.random.randint(jax.random.fold_in(key, axis), (), 0, length) for axis, length in enumerate(values.shape)]
        where[longest] = (where[longest] + shift) % values.shape[longest]
        spots.append(tuple(where))
    return values.at[spots[0]].set(low).at[spots[1]].set(top_value)


def raised(values, own_key, source, target, blocks, factor):
    def block_of(axis_at):
        return (jnp.arange(values.shape[axis_at]) // (values.shape[axis_at] // blocks)).reshape((-1,) + (1,) * (values.ndim - 1 - axis_at))

    near = jax.random.permutation(own_key, blocks)[block_of(target)]
    other_side = (block_of(target) + blocks // 2) % blocks
    return jnp.where((block_of(source) == near) | (block_of(source) == other_side), factor * values, values)


def levels(own_key, dims, cuts, smallest, high):
    loudness, own = 1.0, jax.random.fold_in(own_key, 6)
    for dim, blocks in cuts:
        draws = jnp.exp(jax.random.uniform(jax.random.fold_in(own, dim), (blocks,), jnp.float32, smallest / len(cuts), high / len(cuts)))
        loudness = loudness * jnp.repeat(draws, dims[dim] // blocks).reshape([-1 if axis == dim else 1 for axis in range(len(dims))])
    return loudness


def noise(own_key, shape, deviation, reach, cuts=(), kind=jnp.bfloat16):
    result = deviation * jax.random.normal(own_key, shape, jnp.float32)
    if cuts:
        result = result * levels(own_key, shape, cuts, -0.22, 0.18)
    return jnp.clip(result, -reach, reach).astype(kind)


def gaussian_with(key, shape, scale, bound, cuts, heavy, kind=jnp.bfloat16):
    drawn = scale * jax.random.normal(key, shape, jnp.float32)
    if cuts:
        drawn = drawn * levels(key, shape, cuts, -0.22, 0.18)
    return jnp.clip(raised(drawn, jax.random.fold_in(key, 3), *heavy), -bound, bound).astype(kind)


def setup_inputs(seed: int = 0) -> dict:
    seeds = jax.random.split(jax.random.key(seed), 10)
    return {
        "queries": noise(seeds[0], (SEQUENCE_TOKENS, HK * DK), 1.0, 6.0, ((0, 32), (1, 16))),
        "key_rows": noise(seeds[1], (SEQUENCE_TOKENS, HK * DK), 1.0, 6.0, ((0, 32), (1, 16))),
        "value_rows": noise(seeds[2], (SEQUENCE_TOKENS, VALUE_HEAD_COUNT * DV), 1.0, 6.0, ((0, 32), (1, 16))),
        "out_gate": noise(seeds[3], (SEQUENCE_TOKENS, VALUE_HEAD_COUNT * DV), 1.0, 6.0, ((0, 32), (1, 16))),
        "write_rate": draw_write_rate(jax.random.fold_in(seeds[9], 71), 0),
        "log_gate": draw_log_gate(jax.random.fold_in(seeds[9], 71), 0),
        "doc_start": place_ends((jax.random.randint(seeds[6], (SEQUENCE_TOKENS,), 0, 16 * TOK_DEV) < 1).astype(jnp.int32), jax.random.fold_in(seeds[6], 1), 0, 1),
        "norm_gain": jnp.clip(1.0 + 0.18 * jax.random.normal(seeds[7], (DV,), jnp.float32), 0.1, 1.9),
        "out_weight": gaussian_with(seeds[8], (VALUE_HEAD_COUNT * DV, D), (VALUE_HEAD_COUNT * DV) ** -0.5, 0.125, ((0, 16),), (0, 1, 16, 2.0)),
    }


highest = lax.Precision.HIGHEST

def unit_rows(values):
    return values * lax.rsqrt(lax.optimization_barrier(jnp.sum(values * values, axis=-1, keepdims=True)) + 1e-06)

def block_parts(queries, keys, values, rates, logs, starts):
    cumlog = jnp.cumsum(logs, axis=-1)
    resets = jnp.cumsum(starts, axis=-1)
    token_positions = jnp.arange(SPAN)
    lower_tri = token_positions[:, None] >= token_positions[None, :]
    same_doc = (resets[..., :, None] == resets[..., None, :]) & lower_tri
    log_gap = cumlog[..., :, None] - cumlog[..., None, :]
    decays = jnp.where(same_doc, jnp.exp(jnp.where(same_doc, log_gap, 0.0)), 0.0)
    last_log = cumlog[..., -1:]
    head_keep = jnp.exp(cumlog) * (resets == 0.0)
    tail_keep = jnp.exp(last_log - cumlog) * (resets == resets[..., -1:])
    whole_keep = jnp.exp(cumlog[..., -1]) * (resets[..., -1] == 0.0)
    identity = jnp.eye(SPAN, dtype=jnp.float32)
    key_inner = jnp.einsum('...ik,...jk->...ij', keys, keys, precision=highest)
    coupling = rates[..., :, None] * key_inner * decays * (1.0 - identity)
    inverse = identity - coupling
    powered = coupling
    extent = 1
    while 2 * extent < SPAN:
        powered = jnp.matmul(powered, powered, precision=highest)
        inverse = jnp.matmul(inverse, identity + powered, precision=highest)
        extent = extent * 2
    erase_keys = jnp.matmul(inverse, (rates * head_keep)[..., None] * keys, precision=highest)
    write_vals = jnp.matmul(inverse, rates[..., None] * values, precision=highest)
    scores = jnp.einsum('...ik,...jk->...ij', queries, keys, precision=highest) * decays
    return (queries, keys, erase_keys, write_vals, scores, head_keep, tail_keep, whole_keep)

def state_terms(parts, states):
    queries, keys, erase_keys, write_vals, scores, head_keep, tail_keep, whole_keep = parts
    seen = jnp.einsum('...ck,...vk->...cv', queries, states, precision=highest)
    erased = jnp.einsum('...ck,...vk->...cv', erase_keys, states, precision=highest)
    return (head_keep[..., None] * seen - jnp.matmul(scores, erased, precision=highest), erased)

def block_step(parts, state_now):
    queries, keys, erase_keys, write_vals, scores, head_keep, tail_keep, whole_keep = parts
    terms, erased = state_terms(parts, state_now)
    output = terms + jnp.matmul(scores, write_vals, precision=highest)
    fresh_vals = write_vals - erased
    state_next = whole_keep[..., None, None] * state_now + jnp.einsum('...cv,...ck->...vk', tail_keep[..., None] * fresh_vals, keys, precision=highest)
    return (output, state_next)

def reference(queries, key_rows, value_rows, out_gate, write_rate, log_gate, doc_start, norm_gain, out_weight):
    per_key = VALUE_HEAD_COUNT // HK
    blocks = SEQUENCE_TOKENS // SPAN
    query_unit = unit_rows(queries.astype(jnp.float32).reshape(SEQUENCE_TOKENS, HK, DK))
    key_unit = unit_rows(key_rows.astype(jnp.float32).reshape(SEQUENCE_TOKENS, HK, DK))
    value_all = value_rows.astype(jnp.float32).reshape(SEQUENCE_TOKENS, VALUE_HEAD_COUNT, DV)
    starts = doc_start.astype(jnp.float32).reshape(blocks, SPAN)

    def one_head(head_index):
        key_index = head_index // per_key
        query_head = jnp.take(query_unit, key_index, axis=1).reshape(blocks, SPAN, DK)
        key_head = jnp.take(key_unit, key_index, axis=1).reshape(blocks, SPAN, DK)
        value_head = jnp.take(value_all, head_index, axis=1).reshape(blocks, SPAN, DV)
        rates = jnp.take(write_rate, head_index, axis=0).reshape(blocks, SPAN)
        logs = jnp.take(log_gate, head_index, axis=0).reshape(blocks, SPAN)
        parts = block_parts(query_head, key_head, value_head, rates, logs, starts)

        def advance(state_now, inputs_now):
            output, state_next = block_step(inputs_now, state_now)
            return (state_next, output)
        final_state, outputs = lax.scan(advance, jnp.zeros((DV, DK), jnp.float32), parts)
        return outputs.reshape(SEQUENCE_TOKENS, DV)
    attended = jnp.transpose(lax.map(one_head, jnp.arange(VALUE_HEAD_COUNT, dtype=jnp.int32)), (1, 0, 2))
    gate_vals = out_gate.astype(jnp.float32).reshape(SEQUENCE_TOKENS, VALUE_HEAD_COUNT, DV)
    scale_rows = lax.rsqrt(lax.optimization_barrier(jnp.mean(attended * attended, axis=-1, keepdims=True)) + 1e-06)
    normed = (attended * scale_rows * norm_gain * jax.nn.silu(gate_vals)).astype(jnp.bfloat16)
    normed = normed.reshape(SEQUENCE_TOKENS, VALUE_HEAD_COUNT * DV)
    group_rows = VALUE_HEAD_COUNT * DV // N_HEAD

    def add_group(total, group_index):
        piece = lax.dynamic_slice_in_dim(normed, group_index * group_rows, group_rows, 1)
        weight_rows = lax.dynamic_slice_in_dim(out_weight, group_index * group_rows, group_rows, 0)
        partial_sum = jnp.dot(piece, weight_rows, preferred_element_type=jnp.float32).astype(jnp.bfloat16)
        partial_sum = lax.optimization_barrier(partial_sum)
        return (total + partial_sum.astype(jnp.float32), None)
    mixed, unused = lax.scan(add_group, jnp.zeros((SEQUENCE_TOKENS, D), jnp.float32), jnp.arange(N_HEAD, dtype=jnp.int32))
    return mixed.astype(jnp.bfloat16)
```

```python
import jax
import jax.numpy as jnp
from jax import lax
from jax.experimental import pallas as pl
from jax.experimental.pallas import tpu as pltpu
from jax.sharding import PartitionSpec as P

W = 128
NX, NZ, NY = 4, 8, 8
MSG_ROWS = W + 16
PIECES = 4
f32, bf16 = jnp.float32, jnp.bfloat16
MESH = pl.DeviceIdType.MESH


def dot(a, b):
    return jnp.dot(a, b, preferred_element_type=f32)


def dot_t(a, b):
    return lax.dot_general(a, b, (((1,), (1,)), ((), ())), preferred_element_type=f32)


def split3(x):
    hi = x.astype(bf16)
    rest = x - hi.astype(f32)
    mid = rest.astype(bf16)
    low = (rest - mid.astype(f32)).astype(bf16)
    return hi, mid, low


def local_kernel(
    q_ref, k_ref, v_ref, rate_ref, log_ref, start_ref, qeff_ref, att_ref, msg_ref, rows, cols, y_ref, gam_ref
):
    chunks = q_ref.shape[0] // W
    row = lax.broadcasted_iota(jnp.int32, (W, W), 0)
    col = lax.broadcasted_iota(jnp.int32, (W, W), 1)
    lower = row >= col
    eye = row == col

    rows[...] = jnp.zeros_like(rows)
    for c in range(chunks):
        here = slice(c * W, (c + 1) * W)
        rows[8 * c : 8 * c + 2, :] = log_ref[:, here]
        rows[8 * c + 2 : 8 * c + 3, :] = start_ref[c : c + 1, :].astype(f32)
        rows[8 * c + 3 : 8 * c + 5, :] = rate_ref[:, here]
    raw = rows[...]
    upper = (row <= col).astype(f32)
    summed = jnp.dot(raw, upper, precision=lax.Precision.HIGHEST, preferred_element_type=f32)
    kind = lax.broadcasted_iota(jnp.int32, raw.shape, 0) % 8
    vectors = jnp.where(kind < 3, summed, raw)
    rows[...] = vectors
    turned = jnp.transpose(vectors)
    for c in range(chunks):
        cols[c] = turned[:, 8 * c : 8 * c + 8]

    y_ref[...] = jnp.zeros_like(y_ref)
    gam_ref[...] = jnp.ones_like(gam_ref)

    def prepare(c):
        start = pl.multiple_of(c * W, W)
        kc = k_ref[pl.ds(start, W), :]
        qc = q_ref[pl.ds(start, W), :]
        vc = v_ref[pl.ds(start, W), :]
        vec_r = rows[pl.ds(pl.multiple_of(c * 8, 8), 8), :]
        vec_c = cols[c]
        kf = kc.astype(f32)
        qf = qc.astype(f32)
        rk_c = lax.rsqrt(jnp.sum(kf * kf, axis=1, keepdims=True) + 1e-6)
        rq_c = lax.rsqrt(jnp.sum(qf * qf, axis=1, keepdims=True) + 1e-6)
        rk_r = jnp.sum(jnp.where(eye, rk_c, 0.0), axis=0, keepdims=True)
        kk = dot_t(kc, kc) * rk_c * rk_r
        qk = dot_t(qc, kc) * rq_c * rk_r
        k_turned = jnp.transpose(kf).astype(bf16)
        reset_r, reset_c = vec_r[2:3], vec_c[:, 2:3]
        same = lower & (reset_r == reset_c)
        reset_last = reset_r[:, W - 1 : W]
        found = []
        for h in range(2):
            g_r, g_c = vec_r[h : h + 1], vec_c[:, h : h + 1]
            b_r, b_c = vec_r[3 + h : 4 + h], vec_c[:, 3 + h : 4 + h]
            g_last = g_r[:, W - 1 : W]
            decay = jnp.exp(jnp.where(same, g_c - g_r, -1e9))
            coupling = b_c * kk * decay
            inverse = jnp.where(eye, 1.0, jnp.where((row // 2 == col // 2) & lower, -coupling, 0.0))
            found.append([decay, coupling, inverse])
        size = 2
        while size < W:
            block = (row // (2 * size) == col // (2 * size)) & (row // size > col // size)
            for h in range(2):
                decay, coupling, inverse = found[h]
                inv_b = inverse.astype(bf16)
                part = dot(jnp.where(block, coupling, 0.0).astype(bf16), inv_b)
                found[h][2] = inverse - dot(inv_b, part.astype(bf16))
            size *= 2
        results = []
        for h in range(2):
            decay, coupling, inverse = found[h]
            g_r, g_c = vec_r[h : h + 1], vec_c[:, h : h + 1]
            b_r = vec_r[3 + h : 4 + h]
            g_last = g_r[:, W - 1 : W]
            head_r = jnp.where(reset_r == 0.0, jnp.exp(g_r), 0.0)
            head_c = jnp.where(reset_c == 0.0, jnp.exp(g_c), 0.0)
            tail_c = jnp.where(reset_c == reset_last, jnp.exp(g_last - g_c), 0.0)
            whole = jnp.where(reset_last == 0.0, jnp.exp(g_last), 0.0)
            erase = dot((inverse * (b_r * head_r * rk_r)).astype(bf16), kc)
            write = dot((inverse * b_r).astype(bf16), vc[:, h * W : (h + 1) * W])
            both = jnp.concatenate([erase, write], axis=1)
            score = (qk * decay).astype(bf16)
            scored = dot(score, both.astype(bf16))
            reach = qf * (head_c * rq_c) - scored[:, :W]
            moved = dot(k_turned, (both * (tail_c * rk_c)).astype(bf16))
            results.append((reach, scored[:, W:], moved[:, :W], moved[:, W:], whole))
        return results

    def advance(c, results):
        start = pl.multiple_of(c * W, W)
        for h in range(2):
            reach, local_out, fade, fresh, whole = results[h]
            y = y_ref[h]
            gam = gam_ref[h, 0:1, 0:1]
            stacked = jnp.concatenate([fade, reach], axis=0).astype(bf16)
            product = dot(stacked, y.astype(bf16))
            qeff_ref[pl.ds(start, W), h * W : (h + 1) * W] = (
                product[W:, :W] + gam * reach
            ).astype(bf16)
            att_ref[pl.ds(start, W), h * W : (h + 1) * W] = product[W:, W:] + local_out
            y_ref[h] = whole * y - product[:W] + jnp.concatenate([-gam * fade, fresh], axis=1)
            gam_ref[h] = gam_ref[h] * whole

    def body(i, carry):
        ready = [prepare(2 * i), prepare(2 * i + 1)]
        for j in range(2):
            advance(2 * i + j, ready[j])
        return carry

    lax.fori_loop(0, chunks // 2, body, 0)
    for h in range(2):
        msg_ref[h, :W, :] = y_ref[h].astype(bf16)
        gam = jnp.broadcast_to(gam_ref[h, 0:1, 0:1], (16, 2 * W))
        hi, mid, low = split3(gam)
        at = lax.broadcasted_iota(jnp.int32, (16, 2 * W), 0)
        msg_ref[h, W:, :] = jnp.where(
            at == 0, hi.astype(f32), jnp.where(at == 1, mid.astype(f32), jnp.where(at == 2, low.astype(f32), 0.0))
        ).astype(bf16)


def local_part(queries, keys, values, rates, logs, starts):
    tokens = queries.shape[0]
    chunks = tokens // W
    return pl.pallas_call(
        local_kernel,
        out_shape=(
            jax.ShapeDtypeStruct((tokens, 2 * W), bf16),
            jax.ShapeDtypeStruct((tokens, 2 * W), f32),
            jax.ShapeDtypeStruct((2, MSG_ROWS, 2 * W), bf16),
        ),
        in_specs=[pl.BlockSpec(memory_space=pltpu.VMEM)] * 6,
        out_specs=(pl.BlockSpec(memory_space=pltpu.VMEM),) * 3,
        scratch_shapes=[
            pltpu.VMEM((8 * chunks, W), f32),
            pltpu.VMEM((chunks, W, 8), f32),
            pltpu.VMEM((2, W, 2 * W), f32),
            pltpu.VMEM((2, 8, W), f32),
        ],
        compiler_params=pltpu.CompilerParams(vmem_limit_bytes=32 << 20),
    )(queries, keys, values, rates, logs, starts)


def far_kernel(
    sizes, qeff_ref, att_ref, msg_ref, gate_ref, gain_ref, w_ref, out_ref,
    got, before, hop_out, hop_in, weights, normed, sent, came,
    right_s, right_r, left_s, left_r, hop_s, hop_r, w_own, w_s, w_r, n_s, n_r, ring_s, ring_r,
):
    nx, nz, ny = sizes
    seq, head = lax.axis_index("seq"), lax.axis_index("head")
    x, z = seq // nz, lax.rem(seq, nz)
    y, core = head // 2, lax.rem(head, 2)
    half = nz // 2
    step_y = 1 - 2 * core

    def seq_of(x_at, z_at):
        return lax.rem(x_at + nx, nx) * nz + lax.rem(z_at + nz, nz)

    def head_of(y_at, core_at):
        return lax.rem(y_at + ny, ny) * 2 + core_at

    above, below = (seq_of(x, z + 1), head), (seq_of(x, z - 1), head)
    next_row, last_row = (seq_of(x + 1, z), head), (seq_of(x - 1, z), head)
    sibling = (seq, head_of(y, 1 - core))
    ahead, behind = (seq, head_of(y + 1, core)), (seq, head_of(y - 1, core))
    target = (seq, head_of(y + step_y, core))

    barrier = pltpu.get_barrier_semaphore()
    greeted = (above, below, next_row, last_row, sibling, ahead, behind)
    for other in greeted:
        pl.semaphore_signal(barrier, inc=1, device_id=other, device_id_type=MESH)
    pl.semaphore_wait(barrier, len(greeted))

    def remote(src, dst, send, recv, device):
        return pltpu.make_async_remote_copy(
            src_ref=src, dst_ref=dst, send_sem=send, recv_sem=recv, device_id=device, device_id_type=MESH
        )

    def around(t, h, upward):
        owner = lax.rem(z - t + nz, nz) if upward else lax.rem(z + t, nz)
        src = msg_ref.at[h] if t == 0 else got.at[owner, h]
        if upward:
            return remote(src, got.at[owner, h], right_s.at[t, h], right_r.at[t, h], above)
        return remote(src, got.at[owner, h], left_s.at[t, h], left_r.at[t, h], below)

    def wanted(t, h, upward):
        return t < half - 1 or h == (0 if upward else 1)

    for h in range(2):
        for upward in (True, False):
            if wanted(0, h, upward):
                around(0, h, upward).start()

    def weight_copies(d):
        mine = pl.ds(pl.multiple_of((2 * d + core) * W, W), W)
        theirs = pl.ds(pl.multiple_of((2 * d + 1 - core) * W, W), W)
        own = pltpu.make_async_copy(w_ref.at[:, mine], weights.at[d, : 2 * W], w_own.at[d])
        far = remote(w_ref.at[:, theirs], weights.at[d, 2 * W :], w_s.at[d], w_r.at[d], sibling)
        return own, far

    for d in range(ny):
        own, far = weight_copies(d)
        own.start()
        far.start()

    got[z] = msg_ref[...]
    for t in range(1, half):
        for h in range(2):
            for upward in (True, False):
                if wanted(t - 1, h, upward):
                    around(t - 1, h, upward).wait_recv()
                if wanted(t, h, upward):
                    around(t, h, upward).start()
    for h in range(2):
        for upward in (True, False):
            if wanted(half - 1, h, upward):
                around(half - 1, h, upward).wait_recv()

    def gamma_of(rows16):
        return jnp.sum(rows16.astype(f32), axis=0, keepdims=True)

    total = [jnp.zeros((W, 2 * W), f32)] * 2
    gammas = [jnp.ones((1, 2 * W), f32)] * 2
    for at in range(nz):
        for h in range(2):
            before[at, h, :W] = total[h]
            before[at, h, W : W + 8] = jnp.broadcast_to(gammas[h], (8, 2 * W))
            theirs = got[at, h, :W].astype(f32)
            shrink = gamma_of(got[at, h, W:])
            term = jnp.concatenate([gammas[h][:, :W] * theirs[:, :W], theirs[:, W:]], axis=1)
            if at == 0:
                total[h] = term
            else:
                total[h] = (
                    shrink * total[h] + dot(got[at, h, :W, :W], total[h].astype(bf16)) + term
                )
            gammas[h] = gammas[h] * shrink

    def hop(h):
        return remote(hop_out.at[h], hop_in.at[h], hop_s.at[h], hop_r.at[h], next_row)

    @pl.when(x == 0)
    def _():
        hop_in[...] = jnp.zeros_like(hop_in)

    entering = []
    for h in range(2):
        @pl.when(x > 0)
        def _():
            hop(h).wait_recv()

        came_in = hop_in[h]
        wide = came_in.astype(f32)

        @pl.when(x < nx - 1)
        def _():
            hop_out[h] = (
                gammas[h][:, :W] * wide + dot(total[h][:, :W].astype(bf16), came_in) + total[h][:, W:]
            ).astype(bf16)
            hop(h).start()

        prefix = before[z, h, :W]
        kept = before[z, h, W : W + 1]
        entering.append(
            (kept[:, :W] * wide + dot(prefix[:, :W].astype(bf16), came_in) + prefix[:, W:]).astype(bf16)
        )

    pieces = PIECES
    size = qeff_ref.shape[0] // pieces
    gain = gain_ref[...]

    def normed_copy(p):
        return remote(normed.at[0, p], normed.at[1, p], n_s.at[p], n_r.at[p], sibling)

    def make_normed(p):
        here = slice(p * size, (p + 1) * size)
        for h in range(2):
            lanes = slice(h * W, (h + 1) * W)
            attended = att_ref[here, lanes] + dot(qeff_ref[here, lanes], entering[h])
            scale = lax.rsqrt(jnp.mean(attended * attended, axis=1, keepdims=True) + 1e-6)
            gate = gate_ref[here, lanes].astype(f32)
            normed[0, p, :, lanes] = (attended * scale * gain * (gate / (1.0 + jnp.exp(-gate)))).astype(bf16)

    def partial(p, d):
        return dot(normed[0, p], weights[d, : 2 * W]) + dot(normed[1, p], weights[d, 2 * W :])

    def ring(s, p):
        return remote(sent.at[s, p], came.at[s, p], ring_s.at[s, p], ring_r.at[s, p], target)

    def block_of(s):
        return lax.rem(y - step_y * (s + 1) + 2 * ny, ny)

    def first_step(p):
        normed_copy(p).wait_recv()
        sent[0, p] = partial(p, block_of(0)).astype(bf16)
        ring(0, p).start()

    for p in range(pieces):
        make_normed(p)
        normed_copy(p).start()
        if p == 0:
            for d in range(ny):
                own, far = weight_copies(d)
                own.wait()
                far.wait_recv()
        if p > 0:
            first_step(p - 1)
    first_step(pieces - 1)

    def step(s, carry):
        d = block_of(s)
        for p in range(pieces):
            mine = partial(p, d)
            ring(s - 1, p).wait_recv()
            sent[s, p] = (mine + came[s - 1, p].astype(f32)).astype(bf16)
            ring(s, p).start()
        return carry

    lax.fori_loop(1, ny - 1, step, 0)
    for p in range(pieces):
        mine = partial(p, y)
        ring(ny - 2, p).wait_recv()
        out_ref[p * size : (p + 1) * size, :] = (mine + came[ny - 2, p].astype(f32)).astype(bf16)

    for t in range(half):
        for h in range(2):
            for upward in (True, False):
                if wanted(t, h, upward):
                    around(t, h, upward).wait_send()
    for d in range(ny):
        weight_copies(d)[1].wait_send()
    for h in range(2):
        @pl.when(x < nx - 1)
        def _():
            hop(h).wait_send()
    for p in range(pieces):
        normed_copy(p).wait_send()

    def drain(s, carry):
        for p in range(pieces):
            ring(s, p).wait_send()
        return carry

    lax.fori_loop(0, ny - 1, drain, 0)


def far_part(sizes, qeff, att, msg, gate, gain, weight):
    nx, nz, ny = sizes
    tokens = qeff.shape[0]
    half = nz // 2
    size = tokens // PIECES
    vmem = pl.BlockSpec(memory_space=pltpu.VMEM)
    dma = pltpu.SemaphoreType.DMA

    def kernel(*refs):
        far_kernel(sizes, *refs)

    return pl.pallas_call(
        kernel,
        out_shape=jax.ShapeDtypeStruct((tokens, W), bf16),
        in_specs=[vmem, vmem, vmem, vmem, vmem, pl.BlockSpec(memory_space=pl.ANY)],
        out_specs=vmem,
        scratch_shapes=[
            pltpu.VMEM((nz, 2, MSG_ROWS, 2 * W), bf16),
            pltpu.VMEM((nz, 2, W + 8, 2 * W), f32),
            pltpu.VMEM((2, W, W), bf16),
            pltpu.VMEM((2, W, W), bf16),
            pltpu.VMEM((ny, 4 * W, W), bf16),
            pltpu.VMEM((2, PIECES, size, 2 * W), bf16),
            pltpu.VMEM((ny - 1, PIECES, size, W), bf16),
            pltpu.VMEM((ny - 1, PIECES, size, W), bf16),
            dma((half, 2)), dma((half, 2)), dma((half, 2)), dma((half, 2)),
            dma((2,)), dma((2,)),
            dma((ny,)), dma((ny,)), dma((ny,)),
            dma((PIECES,)), dma((PIECES,)),
            dma((ny - 1, PIECES)), dma((ny - 1, PIECES)),
        ],
        compiler_params=pltpu.CompilerParams(
            collective_id=0, has_side_effects=True, vmem_limit_bytes=48 << 20
        ),
    )(qeff, att, msg, gate, gain, weight)


def build(mesh, sizes):
    def local(queries, keys, values, gate, rates, logs, starts, gain, weight):
        qeff, att, msg = local_part(
            queries, keys, values, rates, logs, starts.reshape(-1, W)
        )
        return far_part(sizes, qeff, att, msg, gate, gain.reshape(1, W), weight)

    both = P("seq", "head")
    placed = (both, both, both, both, P("head", "seq"), P("head", "seq"), P("seq"), P(), P("head", None))
    return jax.shard_map(local, mesh=mesh, in_specs=placed, out_specs=both, check_vma=False)


def solution(mesh):
    return build(mesh, (NX, NZ, NY))
```

```python
import jax
import jax.numpy as jnp
from jax import lax
from jax.experimental import pallas as pl
from jax.experimental.pallas import tpu as pltpu
from jax.sharding import PartitionSpec as P

W = 128
NX, NZ, NY = 4, 8, 8
PIECES = 4
GROUP = 4
f32, bf16 = jnp.float32, jnp.bfloat16
MESH = pl.DeviceIdType.MESH


def dot(a, b):
    return jnp.dot(a, b, preferred_element_type=f32)


def dot_t(a, b):
    return lax.dot_general(a, b, (((1,), (1,)), ((), ())), preferred_element_type=f32)


def compose(later, earlier):
    g2, y2 = later
    g1, y1 = earlier
    term = jnp.concatenate([g1 * y2[:, :W], y2[:, W:]], axis=1)
    return g1 * g2, g2 * y1 + dot(y2[:, :W].astype(bf16), y1.astype(bf16)) + term


def iotas():
    return lax.broadcasted_iota(jnp.int32, (W, W), 0), lax.broadcasted_iota(jnp.int32, (W, W), 1)


def gather_vectors(q_ref, k_ref, rate_ref, log_ref, start_ref, rows, cols):
    chunks = k_ref.shape[0] // W
    row, col = iotas()
    eye = row == col
    rows[...] = jnp.zeros_like(rows)
    for c in range(chunks):
        here = slice(c * W, (c + 1) * W)
        rows[8 * c : 8 * c + 2, :] = log_ref[:, here]
        rows[8 * c + 2 : 8 * c + 3, :] = start_ref[c : c + 1, :].astype(f32)
        rows[8 * c + 3 : 8 * c + 5, :] = rate_ref[:, here]
    raw = rows[...]
    upper = (row <= col).astype(f32)
    summed = jnp.dot(raw, upper, precision=lax.Precision.HIGHEST, preferred_element_type=f32)
    kind = lax.broadcasted_iota(jnp.int32, raw.shape, 0) % 8
    vectors = jnp.where(kind < 3, summed, raw)
    rows[...] = vectors
    turned = jnp.transpose(vectors)
    lane = lax.broadcasted_iota(jnp.int32, (W, 8), 1)
    for c in range(chunks):
        here = slice(c * W, (c + 1) * W)
        kf = k_ref[here, :].astype(f32)
        qf = q_ref[here, :].astype(f32)
        rk_c = lax.rsqrt(jnp.sum(kf * kf, axis=1, keepdims=True) + 1e-6)
        rq_c = lax.rsqrt(jnp.sum(qf * qf, axis=1, keepdims=True) + 1e-6)
        rows[8 * c + 5 : 8 * c + 6, :] = jnp.sum(jnp.where(eye, rk_c, 0.0), axis=0, keepdims=True)
        cols[c] = jnp.where(lane == 5, rk_c, jnp.where(lane == 6, rq_c, turned[:, 8 * c : 8 * c + 8]))


def chunk_at(ref, c):
    return ref[pl.ds(pl.multiple_of(c * W, W), W), :]


def vectors_at(rows, cols, c):
    return rows[pl.ds(pl.multiple_of(c * 8, 8), 8), :], cols[c]


def decay_of(vec_r, vec_c, h):
    row, col = iotas()
    same = (row >= col) & (vec_r[2:3] == vec_c[:, 2:3])
    return jnp.exp(jnp.where(same, vec_c[:, h : h + 1] - vec_r[h : h + 1], -1e9))


def odd_rows(values, size):
    return jnp.concatenate([values[at : at + size] for at in range(size, W, 2 * size)], axis=0)


def refine(inverse, coupling, size):
    if size < 8:
        row, col = iotas()
        block = (row // (2 * size) == col // (2 * size)) & (row // size > col // size)
        inv_b = inverse.astype(bf16)
        part = dot(jnp.where(block, coupling, 0.0).astype(bf16), inv_b)
        return inverse - dot(inv_b, part.astype(bf16))
    row = lax.broadcasted_iota(jnp.int32, (W // 2, W), 0)
    col = lax.broadcasted_iota(jnp.int32, (W // 2, W), 1)
    block = 2 * (row // size) == col // size
    left = jnp.where(block, odd_rows(coupling, size), 0.0).astype(bf16)
    part = dot(left, inverse.astype(bf16))
    zeros = jnp.zeros((size, W), f32)
    spread = []
    for at in range(0, W // 2, size):
        spread += [zeros, part[at : at + size]]
    odd = odd_rows(inverse, size)
    odd = odd - dot(odd.astype(bf16), jnp.concatenate(spread, axis=0).astype(bf16))
    mixed = []
    for at in range(0, W // 2, size):
        mixed += [inverse[2 * at : 2 * at + size], odd[at : at + size]]
    return jnp.concatenate(mixed, axis=0)


def shard_map_of(h, i, first, k_ref, v_ref, rows, cols, kk_ref, kt_ref, both_ref, maps_ref, total_ref, gam_ref):
    row, col = iotas()
    found = []
    for j in range(GROUP):
        c = GROUP * i + j
        vec_r, vec_c = vectors_at(rows, cols, c)
        if first:
            kc = chunk_at(k_ref, c)
            kk = dot_t(kc, kc) * vec_c[:, 5:6] * vec_r[5:6]
            kk_ref[c] = kk
            kt_ref[c] = jnp.transpose(kc.astype(f32)).astype(bf16)
        else:
            kk = kk_ref[c]
        coupling = vec_c[:, 3 + h : 4 + h] * kk * decay_of(vec_r, vec_c, h)
        near = jnp.where((row // 2 == col // 2) & (row >= col), -coupling, 0.0)
        found.append([coupling, jnp.where(row == col, 1.0, near)])
    size = 2
    while size < W:
        for j in range(GROUP):
            found[j][1] = refine(found[j][1], found[j][0], size)
        size *= 2
    moves = []
    for j in range(GROUP):
        c = GROUP * i + j
        inverse = found[j][1]
        vec_r, vec_c = vectors_at(rows, cols, c)
        g_r, g_c, b_r, rk_r = vec_r[h : h + 1], vec_c[:, h : h + 1], vec_r[3 + h : 4 + h], vec_r[5:6]
        reset_r, reset_c = vec_r[2:3], vec_c[:, 2:3]
        g_last, reset_last = g_r[:, W - 1 : W], reset_r[:, W - 1 : W]
        head_r = jnp.where(reset_r == 0.0, jnp.exp(g_r), 0.0)
        tail_c = jnp.where(reset_c == reset_last, jnp.exp(g_last - g_c), 0.0)
        whole = jnp.where(reset_last == 0.0, jnp.exp(g_last), 0.0)
        erase = dot((inverse * (b_r * head_r * rk_r)).astype(bf16), chunk_at(k_ref, c))
        values = v_ref[pl.ds(pl.multiple_of(c * W, W), W), h * W : (h + 1) * W]
        write = dot((inverse * b_r).astype(bf16), values)
        both = jnp.concatenate([erase, write], axis=1)
        both_ref[c, h] = both.astype(bf16)
        moves.append((whole, dot(kt_ref[c], (both * (tail_c * vec_c[:, 5:6])).astype(bf16))))
    total, gam = total_ref[h], gam_ref[h, 0:1, :]
    for j in range(GROUP):
        c = GROUP * i + j
        whole, moved = moves[j]
        total_b = total.astype(bf16)
        maps_ref[c, h] = total_b
        gam_ref[h, pl.ds(8 + c, 1), :] = gam
        total = (
            whole * total
            - dot(moved[:, :W].astype(bf16), total_b)
            + jnp.concatenate([-gam * moved[:, :W], moved[:, W:]], axis=1)
        )
        gam = gam * whole
    total_ref[h] = total
    gam_ref[h, 0:1, :] = gam


def token_outputs(c, q_ref, k_ref, rows, cols, both_ref, maps_ref, gam_ref, qeff_ref, att_ref):
    start = pl.multiple_of(c * W, W)
    vec_r, vec_c = vectors_at(rows, cols, c)
    qc = chunk_at(q_ref, c)
    qk = dot_t(qc, chunk_at(k_ref, c)) * vec_c[:, 6:7] * vec_r[5:6]
    for h in range(2):
        both = both_ref[c, h]
        g_c, reset_c = vec_c[:, h : h + 1], vec_c[:, 2:3]
        head_c = jnp.where(reset_c == 0.0, jnp.exp(g_c), 0.0)
        scored = dot((qk * decay_of(vec_r, vec_c, h)).astype(bf16), both)
        reach = qc.astype(f32) * (head_c * vec_c[:, 6:7]) - scored[:, :W]
        product = dot(reach.astype(bf16), maps_ref[c, h])
        lanes = slice(h * W, (h + 1) * W)
        gam = gam_ref[h, pl.ds(8 + c, 1), :]
        qeff_ref[pl.ds(start, W), lanes] = (product[:, :W] + gam * reach).astype(bf16)
        att_ref[pl.ds(start, W), lanes] = product[:, W:] + scored[:, W:]


def layer_kernel(
    sizes, q_hbm, k_hbm, v_hbm, gate_hbm, rate_hbm, log_hbm, start_hbm, gain_hbm, w_ref, out_ref,
    q_ref, k_ref, v_ref, gate_ref, rate_ref, log_ref, start_ref, gain_ref,
    rows, cols, kk_ref, kt_ref, both_ref, maps_ref, total_ref, gam_ref, qeff_ref, att_ref,
    msg, got, shrinks, hop_out, hop_in, weights, normed, sent, came,
    load, right_s, right_r, left_s, left_r, shrink_s, shrink_r, hop_s, hop_r,
    w_own, w_s, w_r, n_s, n_r, ring_s, ring_r,
):
    nx, nz, ny = sizes
    chunks = q_ref.shape[0] // W
    seq, head = lax.axis_index("seq"), lax.axis_index("head")
    x, z = seq // nz, lax.rem(seq, nz)
    y, core = head // 2, lax.rem(head, 2)
    half = nz // 2
    step_y = 1 - 2 * core

    def seq_of(x_at, z_at):
        return lax.rem(x_at + nx, nx) * nz + lax.rem(z_at + nz, nz)

    def head_of(y_at, core_at):
        return lax.rem(y_at + ny, ny) * 2 + core_at

    next_row, last_row = (seq_of(x + 1, z), head), (seq_of(x - 1, z), head)
    sibling = (seq, head_of(y, 1 - core))
    ahead, behind = (seq, head_of(y + 1, core)), (seq, head_of(y - 1, core))
    target = (seq, head_of(y + step_y, core))
    column = [(seq_of(x, z + dz), head) for dz in range(nz)]
    above, below = column[1], column[nz - 1]

    barrier = pltpu.get_barrier_semaphore()
    greeted = (*column[1:], next_row, last_row, sibling, ahead, behind)
    for other in greeted:
        pl.semaphore_signal(barrier, inc=1, device_id=other, device_id_type=MESH)

    pairs = (
        (log_hbm, log_ref), (rate_hbm, rate_ref), (start_hbm, start_ref), (k_hbm, k_ref), (q_hbm, q_ref),
        (v_hbm, v_ref), (gate_hbm, gate_ref), (gain_hbm, gain_ref),
    )
    loads = [pltpu.make_async_copy(src, dst, load.at[n]) for n, (src, dst) in enumerate(pairs)]
    for copy in loads:
        copy.start()

    def remote(src, dst, send, recv, device):
        return pltpu.make_async_remote_copy(
            src_ref=src, dst_ref=dst, send_sem=send, recv_sem=recv, device_id=device, device_id_type=MESH
        )

    def around(t, h, upward):
        owner = lax.rem(z - t + nz, nz) if upward else lax.rem(z + t, nz)
        src = msg.at[h] if t == 0 else got.at[owner, h]
        if upward:
            return remote(src, got.at[owner, h], right_s.at[t, h], right_r.at[t, h], above)
        return remote(src, got.at[owner, h], left_s.at[t, h], left_r.at[t, h], below)

    def ways(t, h):
        return (True, False) if t < half - 1 else ((True,) if h == 0 else (False,))

    def shrink_copy(dz):
        return remote(
            shrinks.at[z], shrinks.at[z], shrink_s.at[dz], shrink_r.at[dz], column[dz]
        )

    def shrink_arrival(dz):
        at = lax.rem(z - dz + nz, nz)
        return remote(shrinks.at[at], shrinks.at[at], shrink_s.at[dz], shrink_r.at[dz], column[dz])

    def weight_copies(d):
        mine = pl.ds(pl.multiple_of((2 * d + core) * W, W), W)
        theirs = pl.ds(pl.multiple_of((2 * d + 1 - core) * W, W), W)
        own = pltpu.make_async_copy(w_ref.at[:, mine], weights.at[d, : 2 * W], w_own.at[d])
        far = remote(w_ref.at[:, theirs], weights.at[d, 2 * W :], w_s.at[d], w_r.at[d], sibling)
        return own, far

    for n in range(5):
        loads[n].wait()
    gather_vectors(q_ref, k_ref, rate_ref, log_ref, start_ref, rows, cols)
    total_ref[...] = jnp.zeros_like(total_ref)
    gam_ref[...] = jnp.ones_like(gam_ref)
    loads[5].wait()

    def work(h, i):
        shard_map_of(
            h, i, h == 0, k_ref, v_ref, rows, cols, kk_ref, kt_ref, both_ref, maps_ref, total_ref, gam_ref
        )

    def outputs(c):
        token_outputs(c, q_ref, k_ref, rows, cols, both_ref, maps_ref, gam_ref, qeff_ref, att_ref)

    def send_own(h):
        msg[h] = total_ref[h].astype(bf16)
        for upward in (True, False):
            around(0, h, upward).start()

    def pass_on(t, h):
        for upward in (True, False):
            around(t - 1, h, upward).wait_recv()
            if upward in ways(t, h):
                around(t, h, upward).start()

    def loop(count, body):
        def wrapped(i, carry):
            body(i)
            return carry

        lax.fori_loop(0, count, wrapped, 0)

    loop(chunks // GROUP, lambda i: work(0, i))
    pl.semaphore_wait(barrier, len(greeted))
    send_own(0)
    loop(chunks // GROUP, lambda i: work(1, i))
    send_own(1)
    shrinks[z] = jnp.concatenate([gam_ref[0, 0:8, :], gam_ref[1, 0:8, :]], axis=0)
    for dz in range(1, nz):
        shrink_copy(dz).start()
    for d in range(ny):
        own, far = weight_copies(d)
        own.start()
        far.start()
    for h in range(2):
        got[z, h] = msg[h]

    for t in range(1, half):
        pass_on(t, 0)
        if t == 1:
            loop(chunks // 2, outputs)
        pass_on(t, 1)
        if t == 1:
            loop(chunks // 2, lambda c: outputs(c + chunks // 2))
    for h in range(2):
        for upward in ways(half - 1, h):
            around(half - 1, h, upward).wait_recv()
    for dz in range(1, nz):
        shrink_arrival(dz).wait_recv()

    def single(at, h):
        return shrinks[at, 8 * h : 8 * h + 1, 0:1], got[at, h].astype(f32)

    zero = jnp.zeros((W, 2 * W), f32)
    whole_row, prefix = [], []
    for h in range(2):
        level = [single(at, h) for at in range(nz)]
        levels = []
        while len(level) > 1:
            levels.append(level)
            level = [compose(level[n + 1], level[n]) for n in range(0, len(level), 2)]
        whole_row.append(level[0])
        ahead_map = None
        for depth in reversed(range(len(levels))):
            here = levels[depth]
            count = lax.shift_right_logical(z, depth)
            gam, mat = jnp.ones((1, 1), f32), zero
            for n in range(0, len(here), 2):
                take = count == n + 1
                gam = jnp.where(take, here[n][0], gam)
                mat = jnp.where(take, here[n][1], mat)
            ahead_map = (gam, mat) if ahead_map is None else compose((gam, mat), ahead_map)
        prefix.append(ahead_map)

    def hop(h):
        return remote(hop_out.at[h], hop_in.at[h], hop_s.at[h], hop_r.at[h], next_row)

    @pl.when(x == 0)
    def _():
        hop_in[...] = jnp.zeros_like(hop_in)

    def enter(state, came_in):
        gam, mat = state
        return (gam * came_in.astype(f32) + dot(mat[:, :W].astype(bf16), came_in) + mat[:, W:]).astype(bf16)

    for h in range(2):
        @pl.when(x > 0)
        def _():
            hop(h).wait_recv()

        @pl.when(x < nx - 1)
        def _():
            hop_out[h] = enter(whole_row[h], hop_in[h])
            hop(h).start()

    entering = [enter(prefix[h], hop_in[h]) for h in range(2)]

    pieces = PIECES
    size = qeff_ref.shape[0] // pieces
    for n in (6, 7):
        loads[n].wait()
    gain = gain_ref[...]

    def normed_copy(p):
        return remote(normed.at[0, p], normed.at[1, p], n_s.at[p], n_r.at[p], sibling)

    def make_normed(p):
        here = slice(p * size, (p + 1) * size)
        for h in range(2):
            lanes = slice(h * W, (h + 1) * W)
            attended = att_ref[here, lanes] + dot(qeff_ref[here, lanes], entering[h])
            scale = lax.rsqrt(jnp.mean(attended * attended, axis=1, keepdims=True) + 1e-6)
            gate = gate_ref[here, lanes].astype(f32)
            normed[0, p, :, lanes] = (attended * scale * gain * (gate / (1.0 + jnp.exp(-gate)))).astype(bf16)

    def partial(p, d):
        return dot(normed[0, p], weights[d, : 2 * W]) + dot(normed[1, p], weights[d, 2 * W :])

    def ring(s, p):
        return remote(sent.at[s, p], came.at[s, p], ring_s.at[s, p], ring_r.at[s, p], target)

    def block_of(s):
        return lax.rem(y - step_y * (s + 1) + 2 * ny, ny)

    def first_step(p):
        normed_copy(p).wait_recv()
        sent[0, p] = partial(p, block_of(0)).astype(bf16)
        ring(0, p).start()

    for p in range(pieces):
        make_normed(p)
        normed_copy(p).start()
        if p == 0:
            for d in range(ny):
                own, far = weight_copies(d)
                own.wait()
                far.wait_recv()
        if p > 0:
            first_step(p - 1)
    first_step(pieces - 1)

    def step(s):
        d = block_of(s)
        for p in range(pieces):
            mine = partial(p, d)
            ring(s - 1, p).wait_recv()
            sent[s, p] = (mine + came[s - 1, p].astype(f32)).astype(bf16)
            ring(s, p).start()

    loop(ny - 2, lambda s: step(s + 1))
    for p in range(pieces):
        mine = partial(p, y)
        ring(ny - 2, p).wait_recv()
        out_ref[p * size : (p + 1) * size, :] = (mine + came[ny - 2, p].astype(f32)).astype(bf16)

    for t in range(half):
        for h in range(2):
            for upward in ways(t, h):
                around(t, h, upward).wait_send()
    for dz in range(1, nz):
        shrink_copy(dz).wait_send()
    for d in range(ny):
        weight_copies(d)[1].wait_send()
    for h in range(2):
        @pl.when(x < nx - 1)
        def _():
            hop(h).wait_send()
    for p in range(pieces):
        normed_copy(p).wait_send()

    def drain(s):
        for p in range(pieces):
            ring(s, p).wait_send()

    loop(ny - 1, drain)


def layer(sizes, *arrays):
    nx, nz, ny = sizes
    tokens = arrays[0].shape[0]
    chunks = tokens // W
    half = nz // 2
    size = tokens // PIECES
    dma = pltpu.SemaphoreType.DMA

    def kernel(*refs):
        layer_kernel(sizes, *refs)

    return pl.pallas_call(
        kernel,
        out_shape=jax.ShapeDtypeStruct((tokens, W), bf16),
        in_specs=[pl.BlockSpec(memory_space=pltpu.MemorySpace.HBM)] * 9,
        out_specs=pl.BlockSpec(memory_space=pltpu.VMEM),
        scratch_shapes=[
            *[pltpu.VMEM(a.shape, a.dtype) for a in arrays[:8]],
            pltpu.VMEM((8 * chunks, W), f32),
            pltpu.VMEM((chunks, W, 8), f32),
            pltpu.VMEM((chunks, W, W), f32),
            pltpu.VMEM((chunks, W, W), bf16),
            pltpu.VMEM((chunks, 2, W, 2 * W), bf16),
            pltpu.VMEM((chunks, 2, W, 2 * W), bf16),
            pltpu.VMEM((2, W, 2 * W), f32),
            pltpu.VMEM((2, 8 + chunks, W), f32),
            pltpu.VMEM((tokens, 2 * W), bf16),
            pltpu.VMEM((tokens, 2 * W), f32),
            pltpu.VMEM((2, W, 2 * W), bf16),
            pltpu.VMEM((nz, 2, W, 2 * W), bf16),
            pltpu.VMEM((nz, 16, W), f32),
            pltpu.VMEM((2, W, W), bf16),
            pltpu.VMEM((2, W, W), bf16),
            pltpu.VMEM((ny, 4 * W, W), bf16),
            pltpu.VMEM((2, PIECES, size, 2 * W), bf16),
            pltpu.VMEM((ny - 1, PIECES, size, W), bf16),
            pltpu.VMEM((ny - 1, PIECES, size, W), bf16),
            dma((8,)),
            dma((half, 2)), dma((half, 2)), dma((half, 2)), dma((half, 2)),
            dma((nz,)), dma((nz,)),
            dma((2,)), dma((2,)),
            dma((ny,)), dma((ny,)), dma((ny,)),
            dma((PIECES,)), dma((PIECES,)),
            dma((ny - 1, PIECES)), dma((ny - 1, PIECES)),
        ],
        compiler_params=pltpu.CompilerParams(
            collective_id=0, has_side_effects=True, vmem_limit_bytes=56 << 20
        ),
    )(*arrays)


def build(mesh, sizes):
    def local(queries, keys, values, gate, rates, logs, starts, gain, weight):
        return layer(
            sizes, queries, keys, values, gate, rates, logs, starts.reshape(-1, W), gain.reshape(1, W), weight
        )

    both = P("seq", "head")
    placed = (both, both, both, both, P("head", "seq"), P("head", "seq"), P("seq"), P(), P("head", None))
    return jax.shard_map(local, mesh=mesh, in_specs=placed, out_specs=both, check_vma=False)


def solution(mesh):
    return build(mesh, (NX, NZ, NY))
```

```python
import jax
import jax.numpy as jnp
from jax import lax
from jax.experimental import pallas as pl
from jax.experimental.pallas import tpu as pltpu
from jax.sharding import PartitionSpec as P

W = 128
NX, NZ, NY = 4, 8, 8
PIECES = 4
GROUP = 4
PARTS = 4
PART_ROWS = 2 * W // PARTS
f32, bf16 = jnp.float32, jnp.bfloat16
MESH = pl.DeviceIdType.MESH


def dot(a, b):
    return jnp.dot(a, b, preferred_element_type=f32)


def dot_t(a, b):
    return lax.dot_general(a, b, (((1,), (1,)), ((), ())), preferred_element_type=f32)


def compose(later, earlier):
    g2, y2 = later
    g1, y1 = earlier
    term = jnp.concatenate([g1 * y2[:, :W], y2[:, W:]], axis=1)
    return g1 * g2, g2 * y1 + dot(y2[:, :W].astype(bf16), y1.astype(bf16)) + term


def iotas():
    return lax.broadcasted_iota(jnp.int32, (W, W), 0), lax.broadcasted_iota(jnp.int32, (W, W), 1)


def gather_vectors(k_ref, rate_ref, log_ref, start_ref, rows, cols):
    chunks = k_ref.shape[0] // W
    row, col = iotas()
    eye = row == col
    rows[...] = jnp.zeros_like(rows)
    for c in range(chunks):
        here = slice(c * W, (c + 1) * W)
        rows[8 * c : 8 * c + 2, :] = log_ref[:, here]
        rows[8 * c + 2 : 8 * c + 3, :] = start_ref[c : c + 1, :].astype(f32)
        rows[8 * c + 3 : 8 * c + 5, :] = rate_ref[:, here]
    raw = rows[...]
    upper = (row <= col).astype(f32)
    summed = jnp.dot(raw, upper, precision=lax.Precision.HIGHEST, preferred_element_type=f32)
    kind = lax.broadcasted_iota(jnp.int32, raw.shape, 0) % 8
    vectors = jnp.where(kind < 3, summed, raw)
    rows[...] = vectors
    turned = jnp.transpose(vectors)
    lane = lax.broadcasted_iota(jnp.int32, (W, 8), 1)
    for c in range(chunks):
        here = slice(c * W, (c + 1) * W)
        kf = k_ref[here, :].astype(f32)
        rk_c = lax.rsqrt(jnp.sum(kf * kf, axis=1, keepdims=True) + 1e-6)
        rows[8 * c + 5 : 8 * c + 6, :] = jnp.sum(jnp.where(eye, rk_c, 0.0), axis=0, keepdims=True)
        cols[c] = jnp.where(lane == 5, rk_c, turned[:, 8 * c : 8 * c + 8])


def chunk_at(ref, c):
    return ref[pl.ds(pl.multiple_of(c * W, W), W), :]


def vectors_at(rows, cols, c):
    return rows[pl.ds(pl.multiple_of(c * 8, 8), 8), :], cols[c]


def decay_of(vec_r, vec_c, h):
    row, col = iotas()
    same = (row >= col) & (vec_r[2:3] == vec_c[:, 2:3])
    return jnp.exp(jnp.where(same, vec_c[:, h : h + 1] - vec_r[h : h + 1], -1e9))


def twin(pair):
    zero = jnp.zeros((pair.shape[0], W), pair.dtype)
    return jnp.concatenate(
        [jnp.concatenate([pair[:, :W], zero], axis=1), jnp.concatenate([zero, pair[:, W:]], axis=1)], axis=0
    )


def refine(inverse, coupling, size):
    row, col = pair_iotas()
    block = (row // (4 * size) == col // (4 * size)) & (row // size > col // size)
    inv_b = inverse.astype(bf16)
    n = dot(inv_b, twin(jnp.where(block, coupling, 0.0).astype(bf16))).astype(bf16)
    squared = dot(n, twin(n)).astype(bf16)
    once = inverse - dot(n, twin(inv_b))
    return once + dot(squared, twin(once.astype(bf16)))


def pair_iotas():
    row = lax.broadcasted_iota(jnp.int32, (W, 2 * W), 0)
    col = lax.broadcasted_iota(jnp.int32, (W, 2 * W), 1)
    return row, lax.rem(col, W)


def shard_maps(i, group, k_ref, v_ref, rows, cols, both_ref, maps_ref, total_ref, gam_ref):
    row, col = pair_iotas()

    def side(parts):
        return jnp.concatenate(parts, axis=1)

    found = []
    for j in range(group):
        c = group * i + j
        vec_r, vec_c = vectors_at(rows, cols, c)
        kc = chunk_at(k_ref, c)
        kk = dot_t(kc, kc) * vec_c[:, 5:6] * vec_r[5:6]
        coupling = side([vec_c[:, 3 + h : 4 + h] * kk * decay_of(vec_r, vec_c, h) for h in range(2)])
        near = jnp.where((row // 2 == col // 2) & (row >= col), -coupling, 0.0)
        found.append([coupling, jnp.where(row == col, 1.0, near)])
    for size in (2, 8, 32):
        for entry in found:
            entry[1] = refine(entry[1], entry[0], size)
    moves = {}
    for j in range(group):
        c = group * i + j
        vec_r, vec_c = vectors_at(rows, cols, c)
        kc = chunk_at(k_ref, c)
        k_turned = jnp.transpose(kc.astype(f32)).astype(bf16)
        inverse = found[j][1]
        rk_r = vec_r[5:6]
        reset_r, reset_c = vec_r[2:3], vec_c[:, 2:3]
        reset_last = reset_r[:, W - 1 : W]
        rates = [vec_r[3 + h : 4 + h] for h in range(2)]
        heads = [jnp.where(reset_r == 0.0, jnp.exp(vec_r[h : h + 1]), 0.0) for h in range(2)]
        scale = side([rates[h] * heads[h] * rk_r for h in range(2)])
        erase = dot((inverse * scale).astype(bf16), twin(side([kc, kc])))
        write = dot((inverse * side(rates)).astype(bf16), twin(chunk_at(v_ref, c)))
        for h in range(2):
            lanes = slice(h * W, (h + 1) * W)
            g_c = vec_c[:, h : h + 1]
            g_last = vec_r[h : h + 1, W - 1 : W]
            tail_c = jnp.where(reset_c == reset_last, jnp.exp(g_last - g_c), 0.0)
            whole = jnp.where(reset_last == 0.0, jnp.exp(g_last), 0.0)
            both = side([erase[:, lanes], write[:, lanes]])
            both_ref[c, h] = both.astype(bf16)
            moves[j, h] = (whole, dot(k_turned, (both * (tail_c * vec_c[:, 5:6])).astype(bf16)))
    totals = [total_ref[h] for h in range(2)]
    gams = [gam_ref[h, 0:1, :] for h in range(2)]
    for j in range(group):
        c = group * i + j
        for h in range(2):
            whole, moved = moves[j, h]
            total, gam = totals[h], gams[h]
            total_b = total.astype(bf16)
            maps_ref[c, h] = total_b
            gam_ref[h, pl.ds(8 + c, 1), :] = gam
            totals[h] = (
                whole * total
                - dot(moved[:, :W].astype(bf16), total_b)
                + jnp.concatenate([-gam * moved[:, :W], moved[:, W:]], axis=1)
            )
            gams[h] = gam * whole
    for h in range(2):
        total_ref[h] = totals[h]
        gam_ref[h, 0:1, :] = gams[h]


def token_outputs(first, count, q_ref, k_ref, rows, cols, both_ref, maps_ref, gam_ref, qeff_ref, att_ref):
    scores = []
    for c in range(first, first + count):
        vec_r, vec_c = vectors_at(rows, cols, c)
        qc = chunk_at(q_ref, c)
        qf = qc.astype(f32)
        rq_c = lax.rsqrt(jnp.sum(qf * qf, axis=1, keepdims=True) + 1e-6)
        qk = dot_t(qc, chunk_at(k_ref, c)) * rq_c * vec_r[5:6]
        scores.append((qf * rq_c, [(qk * decay_of(vec_r, vec_c, h)).astype(bf16) for h in range(2)]))
    scored = [
        [dot(scores[c - first][1][h], both_ref[c, h]) for h in range(2)] for c in range(first, first + count)
    ]
    for c in range(first, first + count):
        here = slice(c * W, (c + 1) * W)
        vec_r, vec_c = vectors_at(rows, cols, c)
        for h in range(2):
            g_c, reset_c = vec_c[:, h : h + 1], vec_c[:, 2:3]
            head_c = jnp.where(reset_c == 0.0, jnp.exp(g_c), 0.0)
            mine = scored[c - first][h]
            reach = scores[c - first][0] * head_c - mine[:, :W]
            product = dot(reach.astype(bf16), maps_ref[c, h])
            lanes = slice(h * W, (h + 1) * W)
            gam = gam_ref[h, 8 + c : 9 + c, :]
            qeff_ref[here, lanes] = (product[:, :W] + gam * reach).astype(bf16)
            att_ref[here, lanes] = product[:, W:] + mine[:, W:]


def layer_kernel(
    sizes, q_hbm, k_hbm, v_hbm, gate_hbm, rate_hbm, log_hbm, start_hbm, gain_hbm, w_ref, out_ref,
    q_ref, k_ref, v_ref, gate_ref, rate_ref, log_ref, start_ref, gain_ref,
    rows, cols, both_ref, maps_ref, total_ref, gam_ref, qeff_ref, att_ref,
    msg, got, shrinks, hop_out, hop_in, weights, normed, sent, came,
    load, right_s, right_r, left_s, left_r, shrink_s, shrink_r, hop_s, hop_r,
    w_own, w_s, w_r, n_s, n_r, ring_s, ring_r,
):
    nx, nz, ny = sizes
    chunks = q_ref.shape[0] // W
    group = min(GROUP, chunks)
    seq, head = lax.axis_index("seq"), lax.axis_index("head")
    x, z = seq // nz, lax.rem(seq, nz)
    y, core = head // 2, lax.rem(head, 2)
    half = nz // 2
    step_y = 1 - 2 * core

    def seq_of(x_at, z_at):
        return lax.rem(x_at + nx, nx) * nz + lax.rem(z_at + nz, nz)

    def head_of(y_at, core_at):
        return lax.rem(y_at + ny, ny) * 2 + core_at

    next_row, last_row = (seq_of(x + 1, z), head), (seq_of(x - 1, z), head)
    sibling = (seq, head_of(y, 1 - core))
    ahead, behind = (seq, head_of(y + 1, core)), (seq, head_of(y - 1, core))
    target = (seq, head_of(y + step_y, core))
    column = [(seq_of(x, z + dz), head) for dz in range(nz)]
    above, below = column[1], column[nz - 1]

    barrier = pltpu.get_barrier_semaphore()
    greeted = (*column[1:], next_row, last_row, sibling, ahead, behind)
    for other in greeted:
        pl.semaphore_signal(barrier, inc=1, device_id=other, device_id_type=MESH)

    pairs = (
        (log_hbm, log_ref), (rate_hbm, rate_ref), (start_hbm, start_ref), (k_hbm, k_ref), (q_hbm, q_ref),
        (v_hbm, v_ref), (gate_hbm, gate_ref), (gain_hbm, gain_ref),
    )
    loads = [pltpu.make_async_copy(src, dst, load.at[n]) for n, (src, dst) in enumerate(pairs)]
    for copy in loads:
        copy.start()

    def remote(src, dst, send, recv, device):
        return pltpu.make_async_remote_copy(
            src_ref=src, dst_ref=dst, send_sem=send, recv_sem=recv, device_id=device, device_id_type=MESH
        )

    def around(t, h, upward):
        owner = lax.rem(z - t + nz, nz) if upward else lax.rem(z + t, nz)
        src = msg.at[h] if t == 0 else got.at[owner, h]
        if upward:
            return remote(src, got.at[owner, h], right_s.at[t, h], right_r.at[t, h], above)
        return remote(src, got.at[owner, h], left_s.at[t, h], left_r.at[t, h], below)

    def ways(t, h):
        return (True, False) if t < half - 1 else ((True,) if h < PARTS // 2 else (False,))

    def shrink_copy(dz):
        return remote(
            shrinks.at[z], shrinks.at[z], shrink_s.at[dz], shrink_r.at[dz], column[dz]
        )

    def shrink_arrival(dz):
        at = lax.rem(z - dz + nz, nz)
        return remote(shrinks.at[at], shrinks.at[at], shrink_s.at[dz], shrink_r.at[dz], column[dz])

    def weight_copies(d):
        mine = pl.ds(pl.multiple_of((2 * d + core) * W, W), W)
        theirs = pl.ds(pl.multiple_of((2 * d + 1 - core) * W, W), W)
        own = pltpu.make_async_copy(w_ref.at[:, mine], weights.at[d, : 2 * W], w_own.at[d])
        far = remote(w_ref.at[:, theirs], weights.at[d, 2 * W :], w_s.at[d], w_r.at[d], sibling)
        return own, far

    for n in range(5):
        loads[n].wait()
    gather_vectors(k_ref, rate_ref, log_ref, start_ref, rows, cols)
    total_ref[...] = jnp.zeros_like(total_ref)
    gam_ref[...] = jnp.ones_like(gam_ref)
    loads[5].wait()

    def work(i):
        shard_maps(i, group, k_ref, v_ref, rows, cols, both_ref, maps_ref, total_ref, gam_ref)

    def outputs(first, count):
        token_outputs(first, count, q_ref, k_ref, rows, cols, both_ref, maps_ref, gam_ref, qeff_ref, att_ref)

    def pass_on(t, h):
        for upward in (True, False):
            around(t - 1, h, upward).wait_recv()
            if upward in ways(t, h):
                around(t, h, upward).start()

    def loop(count, body):
        def wrapped(i, carry):
            body(i)
            return carry

        lax.fori_loop(0, count, wrapped, 0)

    loop(chunks // group, work)
    pl.semaphore_wait(barrier, len(greeted))
    for part in range(PARTS):
        h, rows_at = part // (PARTS // 2), part % (PARTS // 2) * PART_ROWS
        msg[part] = total_ref[h, rows_at : rows_at + PART_ROWS].astype(bf16)
        for upward in (True, False):
            around(0, part, upward).start()
    shrinks[z] = jnp.concatenate([gam_ref[0, 0:8, :], gam_ref[1, 0:8, :]], axis=0)
    for dz in range(1, nz):
        shrink_copy(dz).start()
    for d in range(ny):
        own, far = weight_copies(d)
        own.start()
        far.start()
    got[z] = msg[...]

    shares = [chunks * n // (half - 1) for n in range(half)] if half > 1 else [0, chunks]
    for t in range(1, half):
        outputs(shares[t - 1], shares[t] - shares[t - 1])
        for part in range(PARTS):
            pass_on(t, part)
    for part in range(PARTS):
        for upward in ways(half - 1, part):
            around(half - 1, part, upward).wait_recv()
    for dz in range(1, nz):
        shrink_arrival(dz).wait_recv()

    def single(at, h):
        pair = [got[at, n] for n in range(h * PARTS // 2, (h + 1) * PARTS // 2)]
        return shrinks[at, 8 * h : 8 * h + 1, 0:1], jnp.concatenate(pair, axis=0).astype(f32)

    zero = jnp.zeros((W, 2 * W), f32)
    whole_row, prefix = [], []
    for h in range(2):
        level = [single(at, h) for at in range(nz)]
        levels = []
        while len(level) > 1:
            levels.append(level)
            level = [compose(level[n + 1], level[n]) for n in range(0, len(level), 2)]
        whole_row.append(level[0])
        ahead_map = None
        for depth in reversed(range(len(levels))):
            here = levels[depth]
            count = lax.shift_right_logical(z, depth)
            gam, mat = jnp.ones((1, 1), f32), zero
            for n in range(0, len(here), 2):
                take = count == n + 1
                gam = jnp.where(take, here[n][0], gam)
                mat = jnp.where(take, here[n][1], mat)
            ahead_map = (gam, mat) if ahead_map is None else compose((gam, mat), ahead_map)
        prefix.append(ahead_map)

    def hop(h):
        return remote(hop_out.at[h], hop_in.at[h], hop_s.at[h], hop_r.at[h], next_row)

    @pl.when(x == 0)
    def _():
        hop_in[...] = jnp.zeros_like(hop_in)

    def enter(state, came_in):
        gam, mat = state
        return (gam * came_in.astype(f32) + dot(mat[:, :W].astype(bf16), came_in) + mat[:, W:]).astype(bf16)

    for h in range(2):
        @pl.when(x > 0)
        def _():
            hop(h).wait_recv()

        @pl.when(x < nx - 1)
        def _():
            hop_out[h] = enter(whole_row[h], hop_in[h])
            hop(h).start()

    entering = [enter(prefix[h], hop_in[h]) for h in range(2)]

    pieces = PIECES
    size = qeff_ref.shape[0] // pieces
    for n in (6, 7):
        loads[n].wait()
    gain = gain_ref[...]

    def normed_copy(p):
        return remote(normed.at[0, p], normed.at[1, p], n_s.at[p], n_r.at[p], sibling)

    def make_normed(p):
        here = slice(p * size, (p + 1) * size)
        for h in range(2):
            lanes = slice(h * W, (h + 1) * W)
            attended = att_ref[here, lanes] + dot(qeff_ref[here, lanes], entering[h])
            scale = lax.rsqrt(jnp.mean(attended * attended, axis=1, keepdims=True) + 1e-6)
            gate = gate_ref[here, lanes].astype(f32)
            normed[0, p, :, lanes] = (attended * scale * gain * (gate / (1.0 + jnp.exp(-gate)))).astype(bf16)

    def partial(p, d):
        return dot(normed[0, p], weights[d, : 2 * W]) + dot(normed[1, p], weights[d, 2 * W :])

    def ring(s, p):
        return remote(sent.at[s, p], came.at[s, p], ring_s.at[s, p], ring_r.at[s, p], target)

    def block_of(s):
        return lax.rem(y - step_y * (s + 1) + 2 * ny, ny)

    def first_step(p):
        normed_copy(p).wait_recv()
        sent[0, p] = partial(p, block_of(0)).astype(bf16)
        ring(0, p).start()

    for p in range(pieces):
        make_normed(p)
        normed_copy(p).start()
        if p == 0:
            for d in range(ny):
                own, far = weight_copies(d)
                own.wait()
                far.wait_recv()
        if p > 0:
            first_step(p - 1)
    first_step(pieces - 1)

    def step(s):
        d = block_of(s)
        for p in range(pieces):
            mine = partial(p, d)
            ring(s - 1, p).wait_recv()
            sent[s, p] = (mine + came[s - 1, p].astype(f32)).astype(bf16)
            ring(s, p).start()

    loop(ny - 2, lambda s: step(s + 1))
    for p in range(pieces):
        mine = partial(p, y)
        ring(ny - 2, p).wait_recv()
        out_ref[p * size : (p + 1) * size, :] = (mine + came[ny - 2, p].astype(f32)).astype(bf16)

    for t in range(half):
        for part in range(PARTS):
            for upward in ways(t, part):
                around(t, part, upward).wait_send()
    for dz in range(1, nz):
        shrink_copy(dz).wait_send()
    for d in range(ny):
        weight_copies(d)[1].wait_send()
    for h in range(2):
        @pl.when(x < nx - 1)
        def _():
            hop(h).wait_send()
    for p in range(pieces):
        normed_copy(p).wait_send()

    def drain(s):
        for p in range(pieces):
            ring(s, p).wait_send()

    loop(ny - 1, drain)


def layer(sizes, *arrays):
    nx, nz, ny = sizes
    tokens = arrays[0].shape[0]
    chunks = tokens // W
    half = nz // 2
    size = tokens // PIECES
    dma = pltpu.SemaphoreType.DMA

    def kernel(*refs):
        layer_kernel(sizes, *refs)

    return pl.pallas_call(
        kernel,
        out_shape=jax.ShapeDtypeStruct((tokens, W), bf16),
        in_specs=[pl.BlockSpec(memory_space=pltpu.MemorySpace.HBM)] * 9,
        out_specs=pl.BlockSpec(memory_space=pltpu.VMEM),
        scratch_shapes=[
            *[pltpu.VMEM(a.shape, a.dtype) for a in arrays[:8]],
            pltpu.VMEM((8 * chunks, W), f32),
            pltpu.VMEM((chunks, W, 8), f32),
            pltpu.VMEM((chunks, 2, W, 2 * W), bf16),
            pltpu.VMEM((chunks, 2, W, 2 * W), bf16),
            pltpu.VMEM((2, W, 2 * W), f32),
            pltpu.VMEM((2, 8 + chunks, W), f32),
            pltpu.VMEM((tokens, 2 * W), bf16),
            pltpu.VMEM((tokens, 2 * W), f32),
            pltpu.VMEM((PARTS, PART_ROWS, 2 * W), bf16),
            pltpu.VMEM((nz, PARTS, PART_ROWS, 2 * W), bf16),
            pltpu.VMEM((nz, 16, W), f32),
            pltpu.VMEM((2, W, W), bf16),
            pltpu.VMEM((2, W, W), bf16),
            pltpu.VMEM((ny, 4 * W, W), bf16),
            pltpu.VMEM((2, PIECES, size, 2 * W), bf16),
            pltpu.VMEM((ny - 1, PIECES, size, W), bf16),
            pltpu.VMEM((ny - 1, PIECES, size, W), bf16),
            dma((8,)),
            dma((half, PARTS)), dma((half, PARTS)), dma((half, PARTS)), dma((half, PARTS)),
            dma((nz,)), dma((nz,)),
            dma((2,)), dma((2,)),
            dma((ny,)), dma((ny,)), dma((ny,)),
            dma((PIECES,)), dma((PIECES,)),
            dma((ny - 1, PIECES)), dma((ny - 1, PIECES)),
        ],
        compiler_params=pltpu.CompilerParams(
            collective_id=0, has_side_effects=True, vmem_limit_bytes=56 << 20
        ),
    )(*arrays)


def build(mesh, sizes):
    def local(queries, keys, values, gate, rates, logs, starts, gain, weight):
        return layer(
            sizes, queries, keys, values, gate, rates, logs, starts.reshape(-1, W), gain.reshape(1, W), weight
        )

    both = P("seq", "head")
    placed = (both, both, both, both, P("head", "seq"), P("head", "seq"), P("seq"), P(), P("head", None))
    return jax.shard_map(local, mesh=mesh, in_specs=placed, out_specs=both, check_vma=False)


def solution(mesh):
    return build(mesh, (NX, NZ, NY))
```

```python
import jax
import jax.numpy as jnp
from jax import lax
from jax.experimental import pallas as pl
from jax.experimental.pallas import tpu as pltpu
from jax.sharding import PartitionSpec as P

W = 128
NX, NZ, NY = 4, 8, 8
PIECES = 4
GROUP = 4
PARTS = 2
PART_ROWS = 2 * W // PARTS
f32, bf16 = jnp.float32, jnp.bfloat16
MESH = pl.DeviceIdType.MESH


def dot(a, b):
    return jnp.dot(a, b, preferred_element_type=f32)


def dot_t(a, b):
    return lax.dot_general(a, b, (((1,), (1,)), ((), ())), preferred_element_type=f32)


def compose(later, earlier):
    g2, y2 = later
    g1, y1 = earlier
    term = jnp.concatenate([g1 * y2[:, :W], y2[:, W:]], axis=1)
    return g1 * g2, g2 * y1 + dot(y2[:, :W].astype(bf16), y1.astype(bf16)) + term


def iotas():
    return lax.broadcasted_iota(jnp.int32, (W, W), 0), lax.broadcasted_iota(jnp.int32, (W, W), 1)


def gather_vectors(k_ref, rate_ref, log_ref, start_ref, rows, cols):
    chunks = k_ref.shape[0] // W
    row, col = iotas()
    eye = row == col
    rows[...] = jnp.zeros_like(rows)
    for c in range(chunks):
        here = slice(c * W, (c + 1) * W)
        rows[8 * c : 8 * c + 2, :] = log_ref[:, here]
        rows[8 * c + 2 : 8 * c + 3, :] = start_ref[c : c + 1, :].astype(f32)
        rows[8 * c + 3 : 8 * c + 5, :] = rate_ref[:, here]
    raw = rows[...]
    upper = (row <= col).astype(f32)
    summed = jnp.dot(raw, upper, precision=lax.Precision.HIGHEST, preferred_element_type=f32)
    kind = lax.broadcasted_iota(jnp.int32, raw.shape, 0) % 8
    vectors = jnp.where(kind < 3, summed, raw)
    rows[...] = vectors
    turned = jnp.transpose(vectors)
    lane = lax.broadcasted_iota(jnp.int32, (W, 8), 1)
    for c in range(chunks):
        here = slice(c * W, (c + 1) * W)
        kf = k_ref[here, :].astype(f32)
        rk_c = lax.rsqrt(jnp.sum(kf * kf, axis=1, keepdims=True) + 1e-6)
        rows[8 * c + 5 : 8 * c + 6, :] = jnp.sum(jnp.where(eye, rk_c, 0.0), axis=0, keepdims=True)
        cols[c] = jnp.where(lane == 5, rk_c, turned[:, 8 * c : 8 * c + 8])


def chunk_at(ref, c):
    return ref[c * W : (c + 1) * W, :] if isinstance(c, int) else ref[pl.ds(pl.multiple_of(c * W, W), W), :]


def vectors_at(rows, cols, c):
    at = slice(8 * c, 8 * c + 8) if isinstance(c, int) else pl.ds(pl.multiple_of(c * 8, 8), 8)
    return rows[at, :], cols[c]


def decay_of(vec_r, vec_c, h):
    row, col = iotas()
    same = (row >= col) & (vec_r[2:3] == vec_c[:, 2:3])
    return jnp.exp(jnp.where(same, vec_c[:, h : h + 1] - vec_r[h : h + 1], -1e9))


def twin(pair):
    zero = jnp.zeros((pair.shape[0], W), pair.dtype)
    return jnp.concatenate(
        [jnp.concatenate([pair[:, :W], zero], axis=1), jnp.concatenate([zero, pair[:, W:]], axis=1)], axis=0
    )


def refine(inverse, coupling, size):
    row, col = pair_iotas()
    block = (row // (4 * size) == col // (4 * size)) & (row // size > col // size)
    inv_b = inverse.astype(bf16)
    n = dot(inv_b, twin(jnp.where(block, coupling, 0.0).astype(bf16))).astype(bf16)
    squared = dot(n, twin(n)).astype(bf16)
    once = inverse - dot(n, twin(inv_b))
    return once + dot(squared, twin(once.astype(bf16)))


def pair_iotas():
    row = lax.broadcasted_iota(jnp.int32, (W, 2 * W), 0)
    col = lax.broadcasted_iota(jnp.int32, (W, 2 * W), 1)
    return row, lax.rem(col, W)


def shard_maps(i, group, k_ref, v_ref, rows, cols, both_ref, maps_ref, total_ref, gam_ref):
    row, col = pair_iotas()

    def side(parts):
        return jnp.concatenate(parts, axis=1)

    found = []
    for j in range(group):
        c = group * i + j
        vec_r, vec_c = vectors_at(rows, cols, c)
        kc = chunk_at(k_ref, c)
        kk = dot_t(kc, kc) * vec_c[:, 5:6] * vec_r[5:6]
        coupling = side([vec_c[:, 3 + h : 4 + h] * kk * decay_of(vec_r, vec_c, h) for h in range(2)])
        near = jnp.where((row // 2 == col // 2) & (row >= col), -coupling, 0.0)
        found.append([coupling, jnp.where(row == col, 1.0, near)])
    for size in (2, 8, 32):
        for entry in found:
            entry[1] = refine(entry[1], entry[0], size)
    moves = {}
    for j in range(group):
        c = group * i + j
        vec_r, vec_c = vectors_at(rows, cols, c)
        kc = chunk_at(k_ref, c)
        k_turned = jnp.transpose(kc.astype(f32)).astype(bf16)
        inverse = found[j][1]
        rk_r = vec_r[5:6]
        reset_r, reset_c = vec_r[2:3], vec_c[:, 2:3]
        reset_last = reset_r[:, W - 1 : W]
        rates = [vec_r[3 + h : 4 + h] for h in range(2)]
        heads = [jnp.where(reset_r == 0.0, jnp.exp(vec_r[h : h + 1]), 0.0) for h in range(2)]
        scale = side([rates[h] * heads[h] * rk_r for h in range(2)])
        erase = dot((inverse * scale).astype(bf16), twin(side([kc, kc])))
        write = dot((inverse * side(rates)).astype(bf16), twin(chunk_at(v_ref, c)))
        for h in range(2):
            lanes = slice(h * W, (h + 1) * W)
            g_c = vec_c[:, h : h + 1]
            g_last = vec_r[h : h + 1, W - 1 : W]
            tail_c = jnp.where(reset_c == reset_last, jnp.exp(g_last - g_c), 0.0)
            whole = jnp.where(reset_last == 0.0, jnp.exp(g_last), 0.0)
            both = side([erase[:, lanes], write[:, lanes]])
            both_ref[c, h] = both.astype(bf16)
            moves[j, h] = (whole, dot(k_turned, (both * (tail_c * vec_c[:, 5:6])).astype(bf16)))
    totals = [total_ref[h] for h in range(2)]
    gams = [gam_ref[h, 0:1, :] for h in range(2)]
    for j in range(group):
        c = group * i + j
        for h in range(2):
            whole, moved = moves[j, h]
            total, gam = totals[h], gams[h]
            total_b = total.astype(bf16)
            maps_ref[c, h] = total_b
            gam_ref[h, pl.ds(8 + c, 1), :] = gam
            totals[h] = (
                whole * total
                - dot(moved[:, :W].astype(bf16), total_b)
                + jnp.concatenate([-gam * moved[:, :W], moved[:, W:]], axis=1)
            )
            gams[h] = gam * whole
    for h in range(2):
        total_ref[h] = totals[h]
        gam_ref[h, 0:1, :] = gams[h]


def token_outputs(first, count, q_ref, k_ref, rows, cols, both_ref, maps_ref, gam_ref, qeff_ref, att_ref):
    scores = []
    for c in range(first, first + count):
        vec_r, vec_c = vectors_at(rows, cols, c)
        qc = chunk_at(q_ref, c)
        qf = qc.astype(f32)
        rq_c = lax.rsqrt(jnp.sum(qf * qf, axis=1, keepdims=True) + 1e-6)
        qk = dot_t(qc, chunk_at(k_ref, c)) * rq_c * vec_r[5:6]
        scores.append((qf * rq_c, [(qk * decay_of(vec_r, vec_c, h)).astype(bf16) for h in range(2)]))
    scored = [
        [dot(scores[c - first][1][h], both_ref[c, h]) for h in range(2)] for c in range(first, first + count)
    ]
    for c in range(first, first + count):
        here = slice(c * W, (c + 1) * W)
        vec_r, vec_c = vectors_at(rows, cols, c)
        for h in range(2):
            g_c, reset_c = vec_c[:, h : h + 1], vec_c[:, 2:3]
            head_c = jnp.where(reset_c == 0.0, jnp.exp(g_c), 0.0)
            mine = scored[c - first][h]
            reach = scores[c - first][0] * head_c - mine[:, :W]
            product = dot(reach.astype(bf16), maps_ref[c, h])
            lanes = slice(h * W, (h + 1) * W)
            gam = gam_ref[h, 8 + c : 9 + c, :]
            qeff_ref[here, lanes] = (product[:, :W] + gam * reach).astype(bf16)
            att_ref[here, lanes] = product[:, W:] + mine[:, W:]


def layer_kernel(
    sizes, q_hbm, k_hbm, v_hbm, gate_hbm, rate_hbm, log_hbm, start_hbm, gain_hbm, w_ref, out_ref,
    q_ref, k_ref, v_ref, gate_ref, rate_ref, log_ref, start_ref, gain_ref,
    rows, cols, both_ref, maps_ref, total_ref, gam_ref, qeff_ref, att_ref,
    msg, got, shrinks, hop_out, hop_in, map_out, map_in, lead, weights, normed, sent, came,
    load, right_s, right_r, left_s, left_r, shrink_s, shrink_r, hop_s, hop_r,
    w_own, w_s, w_r, n_s, n_r, ring_s, ring_r,
):
    nx, nz, ny = sizes
    chunks = q_ref.shape[0] // W
    group = min(GROUP, chunks)
    seq, head = lax.axis_index("seq"), lax.axis_index("head")
    x, z = seq // nz, lax.rem(seq, nz)
    y, core = head // 2, lax.rem(head, 2)
    half = nz // 2
    step_y = 1 - 2 * core

    def seq_of(x_at, z_at):
        return lax.rem(x_at + nx, nx) * nz + lax.rem(z_at + nz, nz)

    def head_of(y_at, core_at):
        return lax.rem(y_at + ny, ny) * 2 + core_at

    next_row, last_row = (seq_of(x + 1, z), head), (seq_of(x - 1, z), head)
    third_row = (seq_of(x + 2, z), head)
    sibling = (seq, head_of(y, 1 - core))
    ahead, behind = (seq, head_of(y + 1, core)), (seq, head_of(y - 1, core))
    target = (seq, head_of(y + step_y, core))
    column = [(seq_of(x, z + dz), head) for dz in range(nz)]
    above, below = column[1], column[nz - 1]

    barrier = pltpu.get_barrier_semaphore()
    greeted = (*column[1:], next_row, last_row, third_row, sibling, ahead, behind)
    for other in greeted:
        pl.semaphore_signal(barrier, inc=1, device_id=other, device_id_type=MESH)

    pairs = (
        (log_hbm, log_ref), (rate_hbm, rate_ref), (start_hbm, start_ref), (k_hbm, k_ref), (q_hbm, q_ref),
        (v_hbm, v_ref), (gate_hbm, gate_ref), (gain_hbm, gain_ref),
    )
    loads = [pltpu.make_async_copy(src, dst, load.at[n]) for n, (src, dst) in enumerate(pairs)]
    for copy in loads:
        copy.start()

    def remote(src, dst, send, recv, device):
        return pltpu.make_async_remote_copy(
            src_ref=src, dst_ref=dst, send_sem=send, recv_sem=recv, device_id=device, device_id_type=MESH
        )

    def around(t, h, upward):
        owner = lax.rem(z - t + nz, nz) if upward else lax.rem(z + t, nz)
        src = msg.at[h] if t == 0 else got.at[owner, h]
        if upward:
            return remote(src, got.at[owner, h], right_s.at[t, h], right_r.at[t, h], above)
        return remote(src, got.at[owner, h], left_s.at[t, h], left_r.at[t, h], below)

    def ways(t, h):
        return (True, False) if t < half - 1 else ((True,) if h < PARTS // 2 else (False,))

    def shrink_copy(dz):
        return remote(shrinks.at[z], shrinks.at[z], shrink_s, shrink_r, column[dz])

    def all_shrinks():
        return remote(shrinks.at[: nz - 1], shrinks.at[: nz - 1], shrink_s, shrink_r, column[1])

    def weight_copies(d):
        mine = pl.ds(pl.multiple_of((2 * d + core) * W, W), W)
        theirs = pl.ds(pl.multiple_of((2 * d + 1 - core) * W, W), W)
        own = pltpu.make_async_copy(w_ref.at[:, mine], weights.at[d, : 2 * W], w_own)
        far = remote(w_ref.at[:, theirs], weights.at[d, 2 * W :], w_s, w_r, sibling)
        return own, far

    def all_weights():
        near, rest = weights.at[:, : 2 * W], weights.at[:, 2 * W :]
        return pltpu.make_async_copy(near, near, w_own), remote(rest, rest, w_s, w_r, sibling)

    for n in range(5):
        loads[n].wait()
    gather_vectors(k_ref, rate_ref, log_ref, start_ref, rows, cols)
    total_ref[...] = jnp.zeros_like(total_ref)
    gam_ref[...] = jnp.ones_like(gam_ref)
    loads[5].wait()

    def work(i):
        shard_maps(i, group, k_ref, v_ref, rows, cols, both_ref, maps_ref, total_ref, gam_ref)

    def outputs(first, count):
        token_outputs(first, count, q_ref, k_ref, rows, cols, both_ref, maps_ref, gam_ref, qeff_ref, att_ref)

    def pass_on(t, h):
        for upward in (True, False):
            around(t - 1, h, upward).wait_recv()
            if upward in ways(t, h):
                around(t, h, upward).start()

    def loop(count, body):
        def wrapped(i, carry):
            body(i)
            return carry

        lax.fori_loop(0, count, wrapped, 0)

    if chunks == group:
        work(0)
    else:
        loop(chunks // group, work)
    pl.semaphore_wait(barrier, len(greeted))
    def send_own(h):
        for n in range(PARTS // 2):
            part = h * PARTS // 2 + n
            msg[part] = total_ref[h, n * PART_ROWS : (n + 1) * PART_ROWS].astype(bf16)
            for upward in (True, False):
                around(0, part, upward).start()

    send_own(0)
    shrinks[z] = jnp.concatenate([gam_ref[0, 0:8, :], gam_ref[1, 0:8, :]], axis=0)
    for dz in range(1, nz):
        shrink_copy(dz).start()
    for d in range(ny):
        own, far = weight_copies(d)
        own.start()
        far.start()
    shares = [chunks * n // half for n in range(half + 1)]
    outputs(0, shares[1])
    for part in range(PARTS // 2):
        for upward in ways(0, part):
            around(0, part, upward).wait_send()
    send_own(1)
    got[z] = msg[...]

    for t in range(1, half):
        for part in range(PARTS):
            pass_on(t, part)
            if part == PARTS // 2 - 1:
                outputs(shares[t], shares[t + 1] - shares[t])
    for part in range(PARTS):
        for upward in ways(half - 1, part):
            around(half - 1, part, upward).wait_recv()
    all_shrinks().wait_recv()

    def single(at, h):
        pair = [got[at, n] for n in range(h * PARTS // 2, (h + 1) * PARTS // 2)]
        return shrinks[at, 8 * h : 8 * h + 1, 0:1], jnp.concatenate(pair, axis=0).astype(f32)

    zero = jnp.zeros((W, 2 * W), f32)
    whole_row, prefix = [], []
    for h in range(2):
        level = [single(at, h) for at in range(nz)]
        levels = []
        while len(level) > 1:
            levels.append(level)
            level = [compose(level[n + 1], level[n]) for n in range(0, len(level), 2)]
        whole_row.append(level[0])
        ahead_map = None
        for depth in reversed(range(len(levels))):
            here = levels[depth]
            count = lax.shift_right_logical(z, depth)
            gam, mat = jnp.ones((1, 1), f32), zero
            for n in range(0, len(here), 2):
                take = count == n + 1
                gam = jnp.where(take, here[n][0], gam)
                mat = jnp.where(take, here[n][1], mat)
            ahead_map = (gam, mat) if ahead_map is None else compose((gam, mat), ahead_map)
        prefix.append(ahead_map)

    def enter(state, came_in):
        gam, mat = state
        return gam * came_in.astype(f32) + dot(mat[:, :W].astype(bf16), came_in) + mat[:, W:]

    def first_hop(h):
        return remote(hop_out.at[h], hop_in.at[h], hop_s.at[h], hop_r.at[h], next_row)

    def map_hop(h):
        return remote(map_out.at[h], map_in.at[h], hop_s.at[2 + h], hop_r.at[2 + h], next_row)

    def second_hop(h, far):
        n = 4 + 2 * far + h
        return remote(hop_out.at[h], hop_in.at[h], hop_s.at[n], hop_r.at[n], third_row if far else next_row)

    if nx not in (2, 4):
        raise ValueError("rows")

    @pl.when(x == 0)
    def _():
        hop_in[...] = jnp.zeros_like(hop_in)
        for h in range(2):
            hop_out[h] = whole_row[h][1][:, W:].astype(bf16)
            first_hop(h).start()

    @pl.when(x == 1)
    def _():
        for h in range(2):
            first_hop(h).wait_recv()
            if nx == 4:
                hop_out[h] = enter(whole_row[h], hop_in[h]).astype(bf16)
                second_hop(h, True).start()
                second_hop(h, False).start()

    if nx == 4:
        @pl.when(x == 2)
        def _():
            for h in range(2):
                gam, mat = whole_row[h]
                map_out[h, :W] = mat.astype(bf16)
                hi = gam.astype(bf16).astype(f32)
                mid = (gam - hi).astype(bf16).astype(f32)
                low = gam - hi - mid
                at = lax.broadcasted_iota(jnp.int32, (16, 2 * W), 0)
                map_out[h, W:] = jnp.where(
                    at == 0, hi, jnp.where(at == 1, mid, jnp.where(at == 2, low, 0.0))
                ).astype(bf16)
                map_hop(h).start()

        @pl.when(x == 3)
        def _():
            for h in range(2):
                map_hop(h).wait_recv()
                gam = jnp.sum(map_in[h, W:].astype(f32), axis=0, keepdims=True)[:, 0:1]
                gam, mat = compose(prefix[h], (gam, map_in[h, :W].astype(f32)))
                lead[h, :W] = mat
                lead[h, W:] = jnp.broadcast_to(gam, (8, 2 * W))
            for h in range(2):
                second_hop(h, True).wait_recv()

        @pl.when(x == 2)
        def _():
            for h in range(2):
                second_hop(h, False).wait_recv()

    @pl.when(x < 3)
    def _():
        for h in range(2):
            lead[h, :W] = prefix[h][1]
            lead[h, W:] = jnp.broadcast_to(prefix[h][0], (8, 2 * W))

    entering = [
        enter((lead[h, W : W + 1, 0:1], lead[h, :W]), hop_in[h]).astype(bf16) for h in range(2)
    ]

    pieces = PIECES
    size = qeff_ref.shape[0] // pieces
    for n in (6, 7):
        loads[n].wait()
    gain = gain_ref[...]

    def normed_copy(p):
        return remote(normed.at[0, p], normed.at[1, p], n_s.at[p], n_r.at[p], sibling)

    def make_normed(p):
        here = slice(p * size, (p + 1) * size)
        for h in range(2):
            lanes = slice(h * W, (h + 1) * W)
            attended = att_ref[here, lanes] + dot(qeff_ref[here, lanes], entering[h])
            scale = lax.rsqrt(jnp.mean(attended * attended, axis=1, keepdims=True) + 1e-6)
            gate = gate_ref[here, lanes].astype(f32)
            normed[0, p, :, lanes] = (attended * scale * gain * (gate / (1.0 + jnp.exp(-gate)))).astype(bf16)

    def partial(p, d):
        return dot(normed[0, p], weights[d, : 2 * W]) + dot(normed[1, p], weights[d, 2 * W :])

    def ring(s, p):
        return remote(sent.at[s, p], came.at[s, p], ring_s.at[p], ring_r.at[s, p], target)

    def block_of(s):
        return lax.rem(y - step_y * (s + 1) + 2 * ny, ny)

    def first_step(p):
        normed_copy(p).wait_recv()
        sent[0, p] = partial(p, block_of(0)).astype(bf16)
        ring(0, p).start()

    for p in range(pieces):
        make_normed(p)
        normed_copy(p).start()
        if p == 0:
            own, far = all_weights()
            own.wait()
            far.wait_recv()
        if p > 0:
            first_step(p - 1)
    first_step(pieces - 1)

    def step(s):
        d = block_of(s)
        for p in range(pieces):
            mine = partial(p, d)
            ring(s - 1, p).wait_recv()
            sent[s, p] = (mine + came[s - 1, p].astype(f32)).astype(bf16)
            ring(s - 1, p).wait_send()
            ring(s, p).start()

    loop(ny - 2, lambda s: step(s + 1))
    for p in range(pieces):
        mine = partial(p, y)
        ring(ny - 2, p).wait_recv()
        out_ref[p * size : (p + 1) * size, :] = (mine + came[ny - 2, p].astype(f32)).astype(bf16)

    for t in range(half):
        for part in range(PARTS):
            for upward in ways(t, part):
                if t > 0 or part >= PARTS // 2:
                    around(t, part, upward).wait_send()
    all_shrinks().wait_send()
    all_weights()[1].wait_send()
    for h in range(2):
        @pl.when(x == 0)
        def _():
            first_hop(h).wait_send()

        if nx == 4:
            @pl.when(x == 1)
            def _():
                second_hop(h, True).wait_send()
                second_hop(h, False).wait_send()

            @pl.when(x == 2)
            def _():
                map_hop(h).wait_send()

    for p in range(pieces):
        normed_copy(p).wait_send()
    for p in range(pieces):
        ring(ny - 2, p).wait_send()


def layer(sizes, *arrays):
    nx, nz, ny = sizes
    tokens = arrays[0].shape[0]
    chunks = tokens // W
    half = nz // 2
    size = tokens // PIECES
    dma = pltpu.SemaphoreType.DMA

    def kernel(*refs):
        layer_kernel(sizes, *refs)

    return pl.pallas_call(
        kernel,
        out_shape=jax.ShapeDtypeStruct((tokens, W), bf16),
        in_specs=[pl.BlockSpec(memory_space=pltpu.MemorySpace.HBM)] * 9,
        out_specs=pl.BlockSpec(memory_space=pltpu.VMEM),
        scratch_shapes=[
            *[pltpu.VMEM(a.shape, a.dtype) for a in arrays[:8]],
            pltpu.VMEM((8 * chunks, W), f32),
            pltpu.VMEM((chunks, W, 8), f32),
            pltpu.VMEM((chunks, 2, W, 2 * W), bf16),
            pltpu.VMEM((chunks, 2, W, 2 * W), bf16),
            pltpu.VMEM((2, W, 2 * W), f32),
            pltpu.VMEM((2, 8 + chunks, W), f32),
            pltpu.VMEM((tokens, 2 * W), bf16),
            pltpu.VMEM((tokens, 2 * W), f32),
            pltpu.VMEM((PARTS, PART_ROWS, 2 * W), bf16),
            pltpu.VMEM((nz, PARTS, PART_ROWS, 2 * W), bf16),
            pltpu.VMEM((nz, 16, W), f32),
            pltpu.VMEM((2, W, W), bf16),
            pltpu.VMEM((2, W, W), bf16),
            pltpu.VMEM((2, W + 16, 2 * W), bf16),
            pltpu.VMEM((2, W + 16, 2 * W), bf16),
            pltpu.VMEM((2, W + 8, 2 * W), f32),
            pltpu.VMEM((ny, 4 * W, W), bf16),
            pltpu.VMEM((2, PIECES, size, 2 * W), bf16),
            pltpu.VMEM((ny - 1, PIECES, size, W), bf16),
            pltpu.VMEM((ny - 1, PIECES, size, W), bf16),
            dma((8,)),
            dma((half, PARTS)), dma((half, PARTS)), dma((half, PARTS)), dma((half, PARTS)),
            dma(()), dma(()),
            dma((8,)), dma((8,)),
            dma(()), dma(()), dma(()),
            dma((PIECES,)), dma((PIECES,)),
            dma((PIECES,)), dma((ny - 1, PIECES)),
        ],
        compiler_params=pltpu.CompilerParams(
            collective_id=0, has_side_effects=True, vmem_limit_bytes=56 << 20
        ),
    )(*arrays)


def build(mesh, sizes):
    def local(queries, keys, values, gate, rates, logs, starts, gain, weight):
        return layer(
            sizes, queries, keys, values, gate, rates, logs, starts.reshape(-1, W), gain.reshape(1, W), weight
        )

    both = P("seq", "head")
    placed = (both, both, both, both, P("head", "seq"), P("head", "seq"), P("seq"), P(), P("head", None))
    return jax.shard_map(local, mesh=mesh, in_specs=placed, out_specs=both, check_vma=False)


def solution(mesh):
    return build(mesh, (NX, NZ, NY))
```

```python
import jax
import jax.numpy as jnp
from jax import lax
from jax.experimental import pallas as pl
from jax.experimental.pallas import tpu as pltpu
from jax.sharding import PartitionSpec as P

W = 128
NX, NZ, NY = 4, 8, 8
PIECES = 4
GROUP = 4
PARTS = 2
PART_ROWS = 2 * W // PARTS
f32, bf16 = jnp.float32, jnp.bfloat16
MESH = pl.DeviceIdType.MESH


def dot(a, b):
    return jnp.dot(a, b, preferred_element_type=f32)


def dot_t(a, b):
    return lax.dot_general(a, b, (((1,), (1,)), ((), ())), preferred_element_type=f32)


def compose(later, earlier):
    g2, y2 = later
    g1, y1 = earlier
    term = jnp.concatenate([g1 * y2[:, :W], y2[:, W:]], axis=1)
    return g1 * g2, g2 * y1 + dot(y2[:, :W].astype(bf16), y1.astype(bf16)) + term


def iotas():
    return lax.broadcasted_iota(jnp.int32, (W, W), 0), lax.broadcasted_iota(jnp.int32, (W, W), 1)


def gather_vectors(k_ref, rate_ref, log_ref, start_ref, rows, cols):
    chunks = k_ref.shape[0] // W
    row, col = iotas()
    eye = row == col
    rows[...] = jnp.zeros_like(rows)
    for c in range(chunks):
        here = slice(c * W, (c + 1) * W)
        rows[8 * c : 8 * c + 2, :] = log_ref[:, here]
        rows[8 * c + 2 : 8 * c + 3, :] = start_ref[c : c + 1, :].astype(f32)
        rows[8 * c + 3 : 8 * c + 5, :] = rate_ref[:, here]
    raw = rows[...]
    upper = (row <= col).astype(f32)
    summed = jnp.dot(raw, upper, precision=lax.Precision.HIGHEST, preferred_element_type=f32)
    kind = lax.broadcasted_iota(jnp.int32, raw.shape, 0) % 8
    vectors = jnp.where(kind < 3, summed, raw)
    rows[...] = vectors
    turned = jnp.transpose(vectors)
    lane = lax.broadcasted_iota(jnp.int32, (W, 8), 1)
    for c in range(chunks):
        here = slice(c * W, (c + 1) * W)
        kf = k_ref[here, :].astype(f32)
        rk_c = lax.rsqrt(jnp.sum(kf * kf, axis=1, keepdims=True) + 1e-6)
        rows[8 * c + 5 : 8 * c + 6, :] = jnp.sum(jnp.where(eye, rk_c, 0.0), axis=0, keepdims=True)
        cols[c] = jnp.where(lane == 5, rk_c, turned[:, 8 * c : 8 * c + 8])


def chunk_at(ref, c):
    return ref[c * W : (c + 1) * W, :] if isinstance(c, int) else ref[pl.ds(pl.multiple_of(c * W, W), W), :]


def vectors_at(rows, cols, c):
    at = slice(8 * c, 8 * c + 8) if isinstance(c, int) else pl.ds(pl.multiple_of(c * 8, 8), 8)
    return rows[at, :], cols[c]


def decay_of(vec_r, vec_c, h):
    row, col = iotas()
    same = (row >= col) & (vec_r[2:3] == vec_c[:, 2:3])
    return jnp.exp(jnp.where(same, vec_c[:, h : h + 1] - vec_r[h : h + 1], -1e9))


def twin(pair):
    zero = jnp.zeros((pair.shape[0], W), pair.dtype)
    return jnp.concatenate(
        [jnp.concatenate([pair[:, :W], zero], axis=1), jnp.concatenate([zero, pair[:, W:]], axis=1)], axis=0
    )


def refine(inverse, coupling, size):
    row, col = pair_iotas()
    block = (row // (4 * size) == col // (4 * size)) & (row // size > col // size)
    inv_b = inverse.astype(bf16)
    n = dot(inv_b, twin(jnp.where(block, coupling, 0.0).astype(bf16))).astype(bf16)
    squared = dot(n, twin(n)).astype(bf16)
    once = inverse - dot(n, twin(inv_b))
    return once + dot(squared, twin(once.astype(bf16)))


def pair_iotas():
    row = lax.broadcasted_iota(jnp.int32, (W, 2 * W), 0)
    col = lax.broadcasted_iota(jnp.int32, (W, 2 * W), 1)
    return row, lax.rem(col, W)


def shard_maps(i, group, k_ref, v_ref, rows, cols, both_ref, maps_ref, total_ref, gam_ref):
    row, col = pair_iotas()

    def side(parts):
        return jnp.concatenate(parts, axis=1)

    found = []
    for j in range(group):
        c = group * i + j
        vec_r, vec_c = vectors_at(rows, cols, c)
        kc = chunk_at(k_ref, c)
        kk = dot_t(kc, kc) * vec_c[:, 5:6] * vec_r[5:6]
        coupling = side([vec_c[:, 3 + h : 4 + h] * kk * decay_of(vec_r, vec_c, h) for h in range(2)])
        near = jnp.where((row // 2 == col // 2) & (row >= col), -coupling, 0.0)
        found.append([coupling, jnp.where(row == col, 1.0, near)])
    for size in (2, 8, 32):
        for entry in found:
            entry[1] = refine(entry[1], entry[0], size)
    moves = {}
    for j in range(group):
        c = group * i + j
        vec_r, vec_c = vectors_at(rows, cols, c)
        kc = chunk_at(k_ref, c)
        k_turned = jnp.transpose(kc.astype(f32)).astype(bf16)
        inverse = found[j][1]
        rk_r = vec_r[5:6]
        reset_r, reset_c = vec_r[2:3], vec_c[:, 2:3]
        reset_last = reset_r[:, W - 1 : W]
        rates = [vec_r[3 + h : 4 + h] for h in range(2)]
        heads = [jnp.where(reset_r == 0.0, jnp.exp(vec_r[h : h + 1]), 0.0) for h in range(2)]
        scale = side([rates[h] * heads[h] * rk_r for h in range(2)])
        erase = dot((inverse * scale).astype(bf16), twin(side([kc, kc])))
        write = dot((inverse * side(rates)).astype(bf16), twin(chunk_at(v_ref, c)))
        for h in range(2):
            lanes = slice(h * W, (h + 1) * W)
            g_c = vec_c[:, h : h + 1]
            g_last = vec_r[h : h + 1, W - 1 : W]
            tail_c = jnp.where(reset_c == reset_last, jnp.exp(g_last - g_c), 0.0)
            whole = jnp.where(reset_last == 0.0, jnp.exp(g_last), 0.0)
            both = side([erase[:, lanes], write[:, lanes]])
            both_ref[c, h] = both.astype(bf16)
            moves[j, h] = (whole, dot(k_turned, (both * (tail_c * vec_c[:, 5:6])).astype(bf16)))
    totals = [total_ref[h] for h in range(2)]
    gams = [gam_ref[h, 0:1, :] for h in range(2)]
    for j in range(group):
        c = group * i + j
        for h in range(2):
            whole, moved = moves[j, h]
            total, gam = totals[h], gams[h]
            total_b = total.astype(bf16)
            maps_ref[c, h] = total_b
            gam_ref[h, pl.ds(8 + c, 1), :] = gam
            totals[h] = (
                whole * total
                - dot(moved[:, :W].astype(bf16), total_b)
                + jnp.concatenate([-gam * moved[:, :W], moved[:, W:]], axis=1)
            )
            gams[h] = gam * whole
    for h in range(2):
        total_ref[h] = totals[h]
        gam_ref[h, 0:1, :] = gams[h]


def token_outputs(
    first, count, q_ref, k_ref, rows, cols, both_ref, maps_ref, gam_ref, qeff_ref, att_ref,
    gate_ref, gain_ref, open_ref,
):
    scores = []
    for c in range(first, first + count):
        vec_r, vec_c = vectors_at(rows, cols, c)
        qc = chunk_at(q_ref, c)
        qf = qc.astype(f32)
        rq_c = lax.rsqrt(jnp.sum(qf * qf, axis=1, keepdims=True) + 1e-6)
        qk = dot_t(qc, chunk_at(k_ref, c)) * rq_c * vec_r[5:6]
        scores.append((qf * rq_c, [(qk * decay_of(vec_r, vec_c, h)).astype(bf16) for h in range(2)]))
    scored = [
        [dot(scores[c - first][1][h], both_ref[c, h]) for h in range(2)] for c in range(first, first + count)
    ]
    for c in range(first, first + count):
        here = slice(c * W, (c + 1) * W)
        vec_r, vec_c = vectors_at(rows, cols, c)
        for h in range(2):
            g_c, reset_c = vec_c[:, h : h + 1], vec_c[:, 2:3]
            head_c = jnp.where(reset_c == 0.0, jnp.exp(g_c), 0.0)
            mine = scored[c - first][h]
            reach = scores[c - first][0] * head_c - mine[:, :W]
            product = dot(reach.astype(bf16), maps_ref[c, h])
            lanes = slice(h * W, (h + 1) * W)
            gam = gam_ref[h, 8 + c : 9 + c, :]
            qeff_ref[here, lanes] = (product[:, :W] + gam * reach).astype(bf16)
            att_ref[here, lanes] = product[:, W:] + mine[:, W:]
            gate = gate_ref[here, lanes].astype(f32)
            open_ref[here, lanes] = gain_ref[...] * (gate / (1.0 + jnp.exp(-gate)))


def layer_kernel(
    sizes, q_hbm, k_hbm, v_hbm, gate_hbm, rate_hbm, log_hbm, start_hbm, gain_hbm, w_ref, out_ref,
    q_ref, k_ref, v_ref, gate_ref, rate_ref, log_ref, start_ref, gain_ref,
    rows, cols, both_ref, maps_ref, total_ref, gam_ref, qeff_ref, att_ref, open_ref,
    msg, got, shrinks, hop_out, hop_in, map_out, map_in, lead, weights, normed, sent, came,
    load, right_s, right_r, left_s, left_r, shrink_s, shrink_r, hop_s, hop_r,
    w_own, w_s, w_r, n_s, n_r, ring_s, ring_r,
):
    nx, nz, ny = sizes
    chunks = q_ref.shape[0] // W
    group = min(GROUP, chunks)
    seq, head = lax.axis_index("seq"), lax.axis_index("head")
    x, z = seq // nz, lax.rem(seq, nz)
    y, core = head // 2, lax.rem(head, 2)
    half = nz // 2
    step_y = 1 - 2 * core

    def seq_of(x_at, z_at):
        return lax.rem(x_at + nx, nx) * nz + lax.rem(z_at + nz, nz)

    def head_of(y_at, core_at):
        return lax.rem(y_at + ny, ny) * 2 + core_at

    next_row, last_row = (seq_of(x + 1, z), head), (seq_of(x - 1, z), head)
    third_row = (seq_of(x + 2, z), head)
    sibling = (seq, head_of(y, 1 - core))
    ahead, behind = (seq, head_of(y + 1, core)), (seq, head_of(y - 1, core))
    target = (seq, head_of(y + step_y, core))
    column = [(seq_of(x, z + dz), head) for dz in range(nz)]
    above, below = column[1], column[nz - 1]

    barrier = pltpu.get_barrier_semaphore()
    greeted = (*column[1:], next_row, last_row, third_row, sibling, ahead, behind)
    for other in greeted:
        pl.semaphore_signal(barrier, inc=1, device_id=other, device_id_type=MESH)

    pairs = (
        (k_hbm, k_ref), (log_hbm, log_ref), (rate_hbm, rate_ref), (start_hbm, start_ref), (q_hbm, q_ref),
        (v_hbm, v_ref), (gate_hbm, gate_ref), (gain_hbm, gain_ref),
    )
    loads = [pltpu.make_async_copy(src, dst, load.at[n]) for n, (src, dst) in enumerate(pairs)]
    for copy in loads:
        copy.start()

    def remote(src, dst, send, recv, device):
        return pltpu.make_async_remote_copy(
            src_ref=src, dst_ref=dst, send_sem=send, recv_sem=recv, device_id=device, device_id_type=MESH
        )

    def around(t, h, upward):
        owner = lax.rem(z - t + nz, nz) if upward else lax.rem(z + t, nz)
        src = msg.at[h] if t == 0 else got.at[owner, h]
        if upward:
            return remote(src, got.at[owner, h], right_s.at[t, h], right_r.at[t, h], above)
        return remote(src, got.at[owner, h], left_s.at[t, h], left_r.at[t, h], below)

    def ways(t, h):
        return (True, False) if t < half - 1 else ((True,) if h < PARTS // 2 else (False,))

    def shrink_copy(dz):
        return remote(shrinks.at[z], shrinks.at[z], shrink_s, shrink_r, column[dz])

    def all_shrinks():
        return remote(shrinks.at[: nz - 1], shrinks.at[: nz - 1], shrink_s, shrink_r, column[1])

    def weight_copies(d):
        mine = pl.ds(pl.multiple_of((2 * d + core) * W, W), W)
        theirs = pl.ds(pl.multiple_of((2 * d + 1 - core) * W, W), W)
        own = pltpu.make_async_copy(w_ref.at[:, mine], weights.at[d, : 2 * W], w_own)
        far = remote(w_ref.at[:, theirs], weights.at[d, 2 * W :], w_s, w_r, sibling)
        return own, far

    def all_weights():
        near, rest = weights.at[:, : 2 * W], weights.at[:, 2 * W :]
        return pltpu.make_async_copy(near, near, w_own), remote(rest, rest, w_s, w_r, sibling)

    for n in range(4):
        loads[n].wait()
    gather_vectors(k_ref, rate_ref, log_ref, start_ref, rows, cols)
    total_ref[...] = jnp.zeros_like(total_ref)
    gam_ref[...] = jnp.ones_like(gam_ref)
    loads[5].wait()

    def work(i):
        shard_maps(i, group, k_ref, v_ref, rows, cols, both_ref, maps_ref, total_ref, gam_ref)

    def outputs(first, count):
        token_outputs(
            first, count, q_ref, k_ref, rows, cols, both_ref, maps_ref, gam_ref, qeff_ref, att_ref,
            gate_ref, gain_ref, open_ref,
        )

    def pass_on(t, h):
        for upward in (True, False):
            around(t - 1, h, upward).wait_recv()
            if upward in ways(t, h):
                around(t, h, upward).start()

    def loop(count, body):
        def wrapped(i, carry):
            body(i)
            return carry

        lax.fori_loop(0, count, wrapped, 0)

    if chunks == group:
        work(0)
    else:
        loop(chunks // group, work)
    pl.semaphore_wait(barrier, len(greeted))
    def send_own(h):
        for n in range(PARTS // 2):
            part = h * PARTS // 2 + n
            msg[part] = total_ref[h, n * PART_ROWS : (n + 1) * PART_ROWS].astype(bf16)
            for upward in (True, False):
                around(0, part, upward).start()

    send_own(0)
    shrinks[z] = jnp.concatenate([gam_ref[0, 0:8, :], gam_ref[1, 0:8, :]], axis=0)
    for dz in range(1, nz):
        shrink_copy(dz).start()
    for d in range(ny):
        own, far = weight_copies(d)
        own.start()
        far.start()
    shares = [chunks * n // half for n in range(half + 1)]
    for n in (4, 6, 7):
        loads[n].wait()
    outputs(0, shares[1])
    for part in range(PARTS // 2):
        for upward in ways(0, part):
            around(0, part, upward).wait_send()
    send_own(1)
    got[z] = msg[...]

    for t in range(1, half):
        for part in range(PARTS):
            pass_on(t, part)
            if part == PARTS // 2 - 1:
                outputs(shares[t], shares[t + 1] - shares[t])
    for part in range(PARTS):
        for upward in ways(half - 1, part):
            around(half - 1, part, upward).wait_recv()
    all_shrinks().wait_recv()

    def single(at, h):
        pair = [got[at, n] for n in range(h * PARTS // 2, (h + 1) * PARTS // 2)]
        return shrinks[at, 8 * h : 8 * h + 1, 0:1], jnp.concatenate(pair, axis=0).astype(f32)

    zero = jnp.zeros((W, 2 * W), f32)
    whole_row, prefix = [], []
    for h in range(2):
        level = [single(at, h) for at in range(nz)]
        levels = []
        while len(level) > 1:
            levels.append(level)
            level = [compose(level[n + 1], level[n]) for n in range(0, len(level), 2)]
        whole_row.append(level[0])
        ahead_map = None
        for depth in reversed(range(len(levels))):
            here = levels[depth]
            count = lax.shift_right_logical(z, depth)
            gam, mat = jnp.ones((1, 1), f32), zero
            for n in range(0, len(here), 2):
                take = count == n + 1
                gam = jnp.where(take, here[n][0], gam)
                mat = jnp.where(take, here[n][1], mat)
            ahead_map = (gam, mat) if ahead_map is None else compose((gam, mat), ahead_map)
        prefix.append(ahead_map)

    def enter(state, came_in):
        gam, mat = state
        return gam * came_in.astype(f32) + dot(mat[:, :W].astype(bf16), came_in) + mat[:, W:]

    def first_hop(h):
        return remote(hop_out.at[h], hop_in.at[h], hop_s.at[h], hop_r.at[h], next_row)

    def map_hop(h):
        return remote(map_out.at[h], map_in.at[h], hop_s.at[2 + h], hop_r.at[2 + h], next_row)

    def second_hop(h, far):
        n = 4 + 2 * far + h
        return remote(hop_out.at[h], hop_in.at[h], hop_s.at[n], hop_r.at[n], third_row if far else next_row)

    if nx not in (2, 4):
        raise ValueError("rows")

    @pl.when(x == 0)
    def _():
        hop_in[...] = jnp.zeros_like(hop_in)
        for h in range(2):
            hop_out[h] = whole_row[h][1][:, W:].astype(bf16)
            first_hop(h).start()

    @pl.when(x == 1)
    def _():
        for h in range(2):
            first_hop(h).wait_recv()
            if nx == 4:
                hop_out[h] = enter(whole_row[h], hop_in[h]).astype(bf16)
                second_hop(h, True).start()
                second_hop(h, False).start()

    if nx == 4:
        @pl.when(x == 2)
        def _():
            for h in range(2):
                gam, mat = whole_row[h]
                map_out[h, :W] = mat.astype(bf16)
                hi = gam.astype(bf16).astype(f32)
                mid = (gam - hi).astype(bf16).astype(f32)
                low = gam - hi - mid
                at = lax.broadcasted_iota(jnp.int32, (16, 2 * W), 0)
                map_out[h, W:] = jnp.where(
                    at == 0, hi, jnp.where(at == 1, mid, jnp.where(at == 2, low, 0.0))
                ).astype(bf16)
                map_hop(h).start()

        @pl.when(x == 3)
        def _():
            for h in range(2):
                map_hop(h).wait_recv()
                gam = jnp.sum(map_in[h, W:].astype(f32), axis=0, keepdims=True)[:, 0:1]
                gam, mat = compose(prefix[h], (gam, map_in[h, :W].astype(f32)))
                lead[h, :W] = mat
                lead[h, W:] = jnp.broadcast_to(gam, (8, 2 * W))
            for h in range(2):
                second_hop(h, True).wait_recv()

        @pl.when(x == 2)
        def _():
            for h in range(2):
                second_hop(h, False).wait_recv()

    @pl.when(x < 3)
    def _():
        for h in range(2):
            lead[h, :W] = prefix[h][1]
            lead[h, W:] = jnp.broadcast_to(prefix[h][0], (8, 2 * W))

    entering = [
        enter((lead[h, W : W + 1, 0:1], lead[h, :W]), hop_in[h]).astype(bf16) for h in range(2)
    ]

    pieces = PIECES
    size = qeff_ref.shape[0] // pieces

    def normed_copy(p):
        return remote(normed.at[0, p], normed.at[1, p], n_s.at[p], n_r.at[p], sibling)

    def make_normed(p):
        here = slice(p * size, (p + 1) * size)
        for h in range(2):
            lanes = slice(h * W, (h + 1) * W)
            attended = att_ref[here, lanes] + dot(qeff_ref[here, lanes], entering[h])
            scale = lax.rsqrt(jnp.mean(attended * attended, axis=1, keepdims=True) + 1e-6)
            normed[0, p, :, lanes] = (attended * scale * open_ref[here, lanes]).astype(bf16)

    def partial(p, d):
        return dot(normed[0, p], weights[d, : 2 * W]) + dot(normed[1, p], weights[d, 2 * W :])

    def ring(s, p):
        return remote(sent.at[s, p], came.at[s, p], ring_s.at[p], ring_r.at[s, p], target)

    def block_of(s):
        return lax.rem(y - step_y * (s + 1) + 2 * ny, ny)

    def first_step(p):
        normed_copy(p).wait_recv()
        sent[0, p] = partial(p, block_of(0)).astype(bf16)
        ring(0, p).start()

    for p in range(pieces):
        make_normed(p)
        normed_copy(p).start()
        if p == 0:
            own, far = all_weights()
            own.wait()
            far.wait_recv()
        if p > 0:
            first_step(p - 1)
    first_step(pieces - 1)

    def step(s):
        d = block_of(s)
        for p in range(pieces):
            mine = partial(p, d)
            ring(s - 1, p).wait_recv()
            sent[s, p] = (mine + came[s - 1, p].astype(f32)).astype(bf16)
            ring(s - 1, p).wait_send()
            ring(s, p).start()

    loop(ny - 2, lambda s: step(s + 1))
    for p in range(pieces):
        mine = partial(p, y)
        ring(ny - 2, p).wait_recv()
        out_ref[p * size : (p + 1) * size, :] = (mine + came[ny - 2, p].astype(f32)).astype(bf16)

    for t in range(half):
        for part in range(PARTS):
            for upward in ways(t, part):
                if t > 0 or part >= PARTS // 2:
                    around(t, part, upward).wait_send()
    all_shrinks().wait_send()
    all_weights()[1].wait_send()
    for h in range(2):
        @pl.when(x == 0)
        def _():
            first_hop(h).wait_send()

        if nx == 4:
            @pl.when(x == 1)
            def _():
                second_hop(h, True).wait_send()
                second_hop(h, False).wait_send()

            @pl.when(x == 2)
            def _():
                map_hop(h).wait_send()

    for p in range(pieces):
        normed_copy(p).wait_send()
    for p in range(pieces):
        ring(ny - 2, p).wait_send()


def layer(sizes, *arrays):
    nx, nz, ny = sizes
    tokens = arrays[0].shape[0]
    chunks = tokens // W
    half = nz // 2
    size = tokens // PIECES
    dma = pltpu.SemaphoreType.DMA

    def kernel(*refs):
        layer_kernel(sizes, *refs)

    return pl.pallas_call(
        kernel,
        out_shape=jax.ShapeDtypeStruct((tokens, W), bf16),
        in_specs=[pl.BlockSpec(memory_space=pltpu.MemorySpace.HBM)] * 9,
        out_specs=pl.BlockSpec(memory_space=pltpu.VMEM),
        scratch_shapes=[
            *[pltpu.VMEM(a.shape, a.dtype) for a in arrays[:8]],
            pltpu.VMEM((8 * chunks, W), f32),
            pltpu.VMEM((chunks, W, 8), f32),
            pltpu.VMEM((chunks, 2, W, 2 * W), bf16),
            pltpu.VMEM((chunks, 2, W, 2 * W), bf16),
            pltpu.VMEM((2, W, 2 * W), f32),
            pltpu.VMEM((2, 8 + chunks, W), f32),
            pltpu.VMEM((tokens, 2 * W), bf16),
            pltpu.VMEM((tokens, 2 * W), f32),
            pltpu.VMEM((tokens, 2 * W), f32),
            pltpu.VMEM((PARTS, PART_ROWS, 2 * W), bf16),
            pltpu.VMEM((nz, PARTS, PART_ROWS, 2 * W), bf16),
            pltpu.VMEM((nz, 16, W), f32),
            pltpu.VMEM((2, W, W), bf16),
            pltpu.VMEM((2, W, W), bf16),
            pltpu.VMEM((2, W + 16, 2 * W), bf16),
            pltpu.VMEM((2, W + 16, 2 * W), bf16),
            pltpu.VMEM((2, W + 8, 2 * W), f32),
            pltpu.VMEM((ny, 4 * W, W), bf16),
            pltpu.VMEM((2, PIECES, size, 2 * W), bf16),
            pltpu.VMEM((ny - 1, PIECES, size, W), bf16),
            pltpu.VMEM((ny - 1, PIECES, size, W), bf16),
            dma((8,)),
            dma((half, PARTS)), dma((half, PARTS)), dma((half, PARTS)), dma((half, PARTS)),
            dma(()), dma(()),
            dma((8,)), dma((8,)),
            dma(()), dma(()), dma(()),
            dma((PIECES,)), dma((PIECES,)),
            dma((PIECES,)), dma((ny - 1, PIECES)),
        ],
        compiler_params=pltpu.CompilerParams(
            collective_id=0, has_side_effects=True, vmem_limit_bytes=48 << 20
        ),
    )(*[pltpu.with_memory_space_constraint(a, pltpu.MemorySpace.HBM) for a in arrays])


def build(mesh, sizes):
    def local(queries, keys, values, gate, rates, logs, starts, gain, weight):
        return layer(
            sizes, queries, keys, values, gate, rates, logs, starts.reshape(-1, W), gain.reshape(1, W), weight
        )

    both = P("seq", "head")
    placed = (both, both, both, both, P("head", "seq"), P("head", "seq"), P("seq"), P(), P("head", None))
    return jax.shard_map(local, mesh=mesh, in_specs=placed, out_specs=both, check_vma=False)


def solution(mesh):
    return build(mesh, (NX, NZ, NY))
```

```python
import jax
import jax.numpy as jnp
from jax import lax
from jax.experimental import pallas as pl
from jax.experimental.pallas import tpu as pltpu
from jax.sharding import PartitionSpec as P

W = 128
NX, NZ, NY = 4, 8, 8
PIECES = 4
PARTS = 2
PART_ROWS = 2 * W // PARTS
f32, bf16 = jnp.float32, jnp.bfloat16
MESH = pl.DeviceIdType.MESH


def dot(a, b):
    return jnp.dot(a, b, preferred_element_type=f32)


def dot_t(a, b):
    return lax.dot_general(a, b, (((1,), (1,)), ((), ())), preferred_element_type=f32)


def compose(later, earlier):
    g2, y2 = later
    g1, y1 = earlier
    term = jnp.concatenate([g1 * y2[:, :W], y2[:, W:]], axis=1)
    return g1 * g2, g2 * y1 + dot(y2[:, :W].astype(bf16), y1.astype(bf16)) + term


def iotas():
    return lax.broadcasted_iota(jnp.int32, (W, W), 0), lax.broadcasted_iota(jnp.int32, (W, W), 1)


def gather_vectors(k_ref, rate_ref, log_ref, start_ref, rows, cols):
    chunks = k_ref.shape[0] // W
    row, col = iotas()
    eye = row == col
    rows[...] = jnp.zeros_like(rows)
    for c in range(chunks):
        here = slice(c * W, (c + 1) * W)
        rows[8 * c : 8 * c + 2, :] = log_ref[:, here]
        rows[8 * c + 2 : 8 * c + 3, :] = start_ref[c : c + 1, :].astype(f32)
        rows[8 * c + 3 : 8 * c + 5, :] = rate_ref[:, here]
    raw = rows[...]
    upper = (row <= col).astype(f32)
    summed = jnp.dot(raw, upper, precision=lax.Precision.HIGHEST, preferred_element_type=f32)
    kind = lax.broadcasted_iota(jnp.int32, raw.shape, 0) % 8
    vectors = jnp.where(kind < 3, summed, raw)
    rows[...] = vectors
    turned = jnp.transpose(vectors)
    lane = lax.broadcasted_iota(jnp.int32, (W, 8), 1)
    for c in range(chunks):
        here = slice(c * W, (c + 1) * W)
        kf = k_ref[here, :].astype(f32)
        rk_c = lax.rsqrt(jnp.sum(kf * kf, axis=1, keepdims=True) + 1e-6)
        rows[8 * c + 5 : 8 * c + 6, :] = jnp.sum(jnp.where(eye, rk_c, 0.0), axis=0, keepdims=True)
        cols[c] = jnp.where(lane == 5, rk_c, turned[:, 8 * c : 8 * c + 8])


def chunk_at(ref, c):
    return ref[c * W : (c + 1) * W, :] if isinstance(c, int) else ref[pl.ds(pl.multiple_of(c * W, W), W), :]


def vectors_at(rows, cols, c):
    at = slice(8 * c, 8 * c + 8) if isinstance(c, int) else pl.ds(pl.multiple_of(c * 8, 8), 8)
    return rows[at, :], cols[c]


def decay_of(vec_r, vec_c, h):
    row, col = iotas()
    same = (row >= col) & (vec_r[2:3] == vec_c[:, 2:3])
    return jnp.exp(jnp.where(same, vec_c[:, h : h + 1] - vec_r[h : h + 1], -1e9))


def twin(pair):
    zero = jnp.zeros((pair.shape[0], W), pair.dtype)
    return jnp.concatenate(
        [jnp.concatenate([pair[:, :W], zero], axis=1), jnp.concatenate([zero, pair[:, W:]], axis=1)], axis=0
    )


def refine(inverse, coupling, size):
    row, col = pair_iotas()
    block = (row // (4 * size) == col // (4 * size)) & (row // size > col // size)
    inv_b = inverse.astype(bf16)
    n = dot(inv_b, twin(jnp.where(block, coupling, 0.0).astype(bf16))).astype(bf16)
    squared = dot(n, twin(n)).astype(bf16)
    once = inverse - dot(n, twin(inv_b))
    return once + dot(squared, twin(once.astype(bf16)))


def pair_iotas():
    row = lax.broadcasted_iota(jnp.int32, (W, 2 * W), 0)
    col = lax.broadcasted_iota(jnp.int32, (W, 2 * W), 1)
    return row, lax.rem(col, W)


def chunk_maps(chunks, k_ref, v_ref, rows, cols, both_ref):
    row, col = pair_iotas()

    def side(parts):
        return jnp.concatenate(parts, axis=1)

    found = []
    for c in range(chunks):
        vec_r, vec_c = vectors_at(rows, cols, c)
        kc = chunk_at(k_ref, c)
        kk = dot_t(kc, kc) * vec_c[:, 5:6] * vec_r[5:6]
        coupling = side([vec_c[:, 3 + h : 4 + h] * kk * decay_of(vec_r, vec_c, h) for h in range(2)])
        near = jnp.where((row // 2 == col // 2) & (row >= col), -coupling, 0.0)
        found.append([coupling, jnp.where(row == col, 1.0, near)])
    for size in (2, 8, 32):
        for entry in found:
            entry[1] = refine(entry[1], entry[0], size)
    moves = {}
    for c in range(chunks):
        vec_r, vec_c = vectors_at(rows, cols, c)
        kc = chunk_at(k_ref, c)
        k_turned = jnp.transpose(kc.astype(f32)).astype(bf16)
        inverse = found[c][1]
        rk_r = vec_r[5:6]
        reset_r, reset_c = vec_r[2:3], vec_c[:, 2:3]
        reset_last = reset_r[:, W - 1 : W]
        rates = [vec_r[3 + h : 4 + h] for h in range(2)]
        heads = [jnp.where(reset_r == 0.0, jnp.exp(vec_r[h : h + 1]), 0.0) for h in range(2)]
        scale = side([rates[h] * heads[h] * rk_r for h in range(2)])
        erase = dot((inverse * scale).astype(bf16), twin(side([kc, kc])))
        write = dot((inverse * side(rates)).astype(bf16), twin(chunk_at(v_ref, c)))
        for h in range(2):
            lanes = slice(h * W, (h + 1) * W)
            g_c = vec_c[:, h : h + 1]
            g_last = vec_r[h : h + 1, W - 1 : W]
            tail_c = jnp.where(reset_c == reset_last, jnp.exp(g_last - g_c), 0.0)
            whole = jnp.where(reset_last == 0.0, jnp.exp(g_last), 0.0)
            both = side([erase[:, lanes], write[:, lanes]])
            both_ref[c, h] = both.astype(bf16)
            moved = dot(k_turned, (both * (tail_c * vec_c[:, 5:6])).astype(bf16))
            moves[c, h] = (whole, side([-moved[:, :W], moved[:, W:]]))
    return moves


def prefix_map(levels, count):
    found = None
    for depth in reversed(range(len(levels))):
        if count >> depth & 1:
            here = levels[depth][(count >> depth) - 1]
            found = here if found is None else compose(here, found)
    return found


def token_outputs(
    first, count, q_ref, k_ref, rows, cols, both_ref, maps_ref, gam_ref, qeff_ref, att_ref,
    gate_ref, gain_ref, open_ref,
):
    scores = []
    for c in range(first, first + count):
        vec_r, vec_c = vectors_at(rows, cols, c)
        qc = chunk_at(q_ref, c)
        qf = qc.astype(f32)
        rq_c = lax.rsqrt(jnp.sum(qf * qf, axis=1, keepdims=True) + 1e-6)
        qk = dot_t(qc, chunk_at(k_ref, c)) * rq_c * vec_r[5:6]
        scores.append((qf * rq_c, [(qk * decay_of(vec_r, vec_c, h)).astype(bf16) for h in range(2)]))
    scored = [
        [dot(scores[c - first][1][h], both_ref[c, h]) for h in range(2)] for c in range(first, first + count)
    ]
    for c in range(first, first + count):
        here = slice(c * W, (c + 1) * W)
        vec_r, vec_c = vectors_at(rows, cols, c)
        for h in range(2):
            g_c, reset_c = vec_c[:, h : h + 1], vec_c[:, 2:3]
            head_c = jnp.where(reset_c == 0.0, jnp.exp(g_c), 0.0)
            mine = scored[c - first][h]
            reach = scores[c - first][0] * head_c - mine[:, :W]
            product = dot(reach.astype(bf16), maps_ref[c, h])
            lanes = slice(h * W, (h + 1) * W)
            gam = gam_ref[h, 8 + c : 9 + c, :]
            qeff_ref[here, lanes] = (product[:, :W] + gam * reach).astype(bf16)
            att_ref[here, lanes] = product[:, W:] + mine[:, W:]
            gate = gate_ref[here, lanes].astype(f32)
            open_ref[here, lanes] = gain_ref[...] * (gate / (1.0 + jnp.exp(-gate)))


def layer_kernel(
    sizes, q_hbm, k_hbm, v_hbm, gate_hbm, rate_hbm, log_hbm, start_hbm, gain_hbm, w_ref, out_ref,
    q_ref, k_ref, v_ref, gate_ref, rate_ref, log_ref, start_ref, gain_ref,
    rows, cols, both_ref, maps_ref, gam_ref, qeff_ref, att_ref, open_ref,
    msg, got, shrinks, hop_out, hop_in, map_out, map_in, lead, weights, normed, sent, came,
    load, right_s, right_r, left_s, left_r, shrink_s, shrink_r, hop_s, hop_r,
    w_own, w_s, w_r, n_s, n_r, ring_s, ring_r,
):
    nx, nz, ny = sizes
    chunks = q_ref.shape[0] // W
    seq, head = lax.axis_index("seq"), lax.axis_index("head")
    x, z = seq // nz, lax.rem(seq, nz)
    y, core = head // 2, lax.rem(head, 2)
    half = nz // 2
    step_y = 1 - 2 * core

    def seq_of(x_at, z_at):
        return lax.rem(x_at + nx, nx) * nz + lax.rem(z_at + nz, nz)

    def head_of(y_at, core_at):
        return lax.rem(y_at + ny, ny) * 2 + core_at

    next_row, last_row = (seq_of(x + 1, z), head), (seq_of(x - 1, z), head)
    third_row = (seq_of(x + 2, z), head)
    sibling = (seq, head_of(y, 1 - core))
    ahead, behind = (seq, head_of(y + 1, core)), (seq, head_of(y - 1, core))
    target = (seq, head_of(y + step_y, core))
    column = [(seq_of(x, z + dz), head) for dz in range(nz)]
    above, below = column[1], column[nz - 1]

    barrier = pltpu.get_barrier_semaphore()
    greeted = (*column[1:], next_row, last_row, third_row, sibling, ahead, behind)
    for other in greeted:
        pl.semaphore_signal(barrier, inc=1, device_id=other, device_id_type=MESH)

    pairs = (
        (k_hbm, k_ref), (log_hbm, log_ref), (rate_hbm, rate_ref), (start_hbm, start_ref), (q_hbm, q_ref),
        (v_hbm, v_ref), (gate_hbm, gate_ref), (gain_hbm, gain_ref),
    )
    loads = [pltpu.make_async_copy(src, dst, load.at[n]) for n, (src, dst) in enumerate(pairs)]
    for copy in loads:
        copy.start()

    def remote(src, dst, send, recv, device):
        return pltpu.make_async_remote_copy(
            src_ref=src, dst_ref=dst, send_sem=send, recv_sem=recv, device_id=device, device_id_type=MESH
        )

    def around(t, h, upward):
        owner = lax.rem(z - t + nz, nz) if upward else lax.rem(z + t, nz)
        src = msg.at[h] if t == 0 else got.at[owner, h]
        if upward:
            return remote(src, got.at[owner, h], right_s.at[t, h], right_r.at[t, h], above)
        return remote(src, got.at[owner, h], left_s.at[t, h], left_r.at[t, h], below)

    def ways(t, h):
        return (True, False) if t < half - 1 else ((True,) if h < PARTS // 2 else (False,))

    def shrink_copy(dz):
        return remote(shrinks.at[z], shrinks.at[z], shrink_s, shrink_r, column[dz])

    def all_shrinks():
        return remote(shrinks.at[: nz - 1], shrinks.at[: nz - 1], shrink_s, shrink_r, column[1])

    def weight_copies(d):
        mine = pl.ds(pl.multiple_of((2 * d + core) * W, W), W)
        theirs = pl.ds(pl.multiple_of((2 * d + 1 - core) * W, W), W)
        own = pltpu.make_async_copy(w_ref.at[:, mine], weights.at[d, : 2 * W], w_own)
        far = remote(w_ref.at[:, theirs], weights.at[d, 2 * W :], w_s, w_r, sibling)
        return own, far

    def all_weights():
        near, rest = weights.at[:, : 2 * W], weights.at[:, 2 * W :]
        return pltpu.make_async_copy(near, near, w_own), remote(rest, rest, w_s, w_r, sibling)

    for n in range(4):
        loads[n].wait()
    gather_vectors(k_ref, rate_ref, log_ref, start_ref, rows, cols)
    loads[5].wait()

    def outputs(first, count):
        token_outputs(
            first, count, q_ref, k_ref, rows, cols, both_ref, maps_ref, gam_ref, qeff_ref, att_ref,
            gate_ref, gain_ref, open_ref,
        )

    def pass_on(t, h):
        for upward in (True, False):
            around(t - 1, h, upward).wait_recv()
            if upward in ways(t, h):
                around(t, h, upward).start()

    def loop(count, body):
        def wrapped(i, carry):
            body(i)
            return carry

        lax.fori_loop(0, count, wrapped, 0)

    moves = chunk_maps(chunks, k_ref, v_ref, rows, cols, both_ref)
    trees = []
    for h in range(2):
        tree = [[moves[c, h] for c in range(chunks)]]
        while len(tree[-1]) > 1:
            last = tree[-1]
            tree.append([compose(last[n + 1], last[n]) for n in range(0, len(last), 2)])
        trees.append(tree)
        gam_ref[h, 0:8, :] = jnp.broadcast_to(tree[-1][0][0], (8, W))
    pl.semaphore_wait(barrier, len(greeted))
    def send_own(h):
        for n in range(PARTS // 2):
            part = h * PARTS // 2 + n
            msg[part] = trees[h][-1][0][1][n * PART_ROWS : (n + 1) * PART_ROWS].astype(bf16)
            for upward in (True, False):
                around(0, part, upward).start()

    send_own(0)
    shrinks[z] = jnp.concatenate([gam_ref[0, 0:8, :], gam_ref[1, 0:8, :]], axis=0)
    for dz in range(1, nz):
        shrink_copy(dz).start()
    for d in range(ny):
        own, far = weight_copies(d)
        own.start()
        far.start()
    shares = [chunks * n // half for n in range(half + 1)]
    for n in (4, 6, 7):
        loads[n].wait()
    for h in range(2):
        maps_ref[0, h] = jnp.zeros((W, 2 * W), bf16)
        gam_ref[h, 8:9, :] = jnp.ones((1, W), f32)
        for c in range(1, chunks):
            gam, mat = prefix_map(trees[h], c)
            maps_ref[c, h] = mat.astype(bf16)
            gam_ref[h, 8 + c : 9 + c, :] = jnp.broadcast_to(gam, (1, W))
    outputs(0, shares[1])
    for part in range(PARTS // 2):
        for upward in ways(0, part):
            around(0, part, upward).wait_send()
    send_own(1)
    got[z] = msg[...]

    for t in range(1, half):
        for part in range(PARTS):
            pass_on(t, part)
            if part == PARTS // 2 - 1:
                outputs(shares[t], shares[t + 1] - shares[t])
    for part in range(PARTS):
        for upward in ways(half - 1, part):
            around(half - 1, part, upward).wait_recv()
    all_shrinks().wait_recv()

    def single(at, h):
        pair = [got[at, n] for n in range(h * PARTS // 2, (h + 1) * PARTS // 2)]
        return shrinks[at, 8 * h : 8 * h + 1, 0:1], jnp.concatenate(pair, axis=0).astype(f32)

    zero = jnp.zeros((W, 2 * W), f32)
    whole_row, prefix = [], []
    for h in range(2):
        level = [single(at, h) for at in range(nz)]
        levels = []
        while len(level) > 1:
            levels.append(level)
            level = [compose(level[n + 1], level[n]) for n in range(0, len(level), 2)]
        whole_row.append(level[0])
        ahead_map = None
        for depth in reversed(range(len(levels))):
            here = levels[depth]
            count = lax.shift_right_logical(z, depth)
            gam, mat = jnp.ones((1, 1), f32), zero
            for n in range(0, len(here), 2):
                take = count == n + 1
                gam = jnp.where(take, here[n][0], gam)
                mat = jnp.where(take, here[n][1], mat)
            ahead_map = (gam, mat) if ahead_map is None else compose((gam, mat), ahead_map)
        prefix.append(ahead_map)

    def enter(state, came_in):
        gam, mat = state
        return gam * came_in.astype(f32) + dot(mat[:, :W].astype(bf16), came_in) + mat[:, W:]

    def first_hop(h):
        return remote(hop_out.at[h], hop_in.at[h], hop_s.at[h], hop_r.at[h], next_row)

    def map_hop(h):
        return remote(map_out.at[h], map_in.at[h], hop_s.at[2 + h], hop_r.at[2 + h], next_row)

    def second_hop(h, far):
        n = 4 + 2 * far + h
        return remote(hop_out.at[h], hop_in.at[h], hop_s.at[n], hop_r.at[n], third_row if far else next_row)

    if nx not in (2, 4):
        raise ValueError("rows")

    @pl.when(x == 0)
    def _():
        hop_in[...] = jnp.zeros_like(hop_in)
        for h in range(2):
            hop_out[h] = whole_row[h][1][:, W:].astype(bf16)
            first_hop(h).start()

    @pl.when(x == 1)
    def _():
        for h in range(2):
            first_hop(h).wait_recv()
            if nx == 4:
                hop_out[h] = enter(whole_row[h], hop_in[h]).astype(bf16)
                second_hop(h, True).start()
                second_hop(h, False).start()

    if nx == 4:
        @pl.when(x == 2)
        def _():
            for h in range(2):
                gam, mat = whole_row[h]
                map_out[h, :W] = mat.astype(bf16)
                hi = gam.astype(bf16).astype(f32)
                mid = (gam - hi).astype(bf16).astype(f32)
                low = gam - hi - mid
                at = lax.broadcasted_iota(jnp.int32, (16, 2 * W), 0)
                map_out[h, W:] = jnp.where(
                    at == 0, hi, jnp.where(at == 1, mid, jnp.where(at == 2, low, 0.0))
                ).astype(bf16)
                map_hop(h).start()

        @pl.when(x == 3)
        def _():
            for h in range(2):
                map_hop(h).wait_recv()
                gam = jnp.sum(map_in[h, W:].astype(f32), axis=0, keepdims=True)[:, 0:1]
                gam, mat = compose(prefix[h], (gam, map_in[h, :W].astype(f32)))
                lead[h, :W] = mat
                lead[h, W:] = jnp.broadcast_to(gam, (8, 2 * W))
            for h in range(2):
                second_hop(h, True).wait_recv()

        @pl.when(x == 2)
        def _():
            for h in range(2):
                second_hop(h, False).wait_recv()

    @pl.when(x < 3)
    def _():
        for h in range(2):
            lead[h, :W] = prefix[h][1]
            lead[h, W:] = jnp.broadcast_to(prefix[h][0], (8, 2 * W))

    entering = [
        enter((lead[h, W : W + 1, 0:1], lead[h, :W]), hop_in[h]).astype(bf16) for h in range(2)
    ]

    pieces = PIECES
    size = qeff_ref.shape[0] // pieces

    def normed_copy(p):
        return remote(normed.at[0, p], normed.at[1, p], n_s.at[p], n_r.at[p], sibling)

    def make_normed(p):
        here = slice(p * size, (p + 1) * size)
        for h in range(2):
            lanes = slice(h * W, (h + 1) * W)
            attended = att_ref[here, lanes] + dot(qeff_ref[here, lanes], entering[h])
            scale = lax.rsqrt(jnp.mean(attended * attended, axis=1, keepdims=True) + 1e-6)
            normed[0, p, :, lanes] = (attended * scale * open_ref[here, lanes]).astype(bf16)

    def partial(p, d):
        return dot(normed[0, p], weights[d, : 2 * W]) + dot(normed[1, p], weights[d, 2 * W :])

    def ring(s, p):
        return remote(sent.at[s, p], came.at[s, p], ring_s.at[p], ring_r.at[s, p], target)

    def block_of(s):
        return lax.rem(y - step_y * (s + 1) + 2 * ny, ny)

    def first_step(p):
        normed_copy(p).wait_recv()
        sent[0, p] = partial(p, block_of(0)).astype(bf16)
        ring(0, p).start()

    for p in range(pieces):
        make_normed(p)
        normed_copy(p).start()
        if p == 0:
            own, far = all_weights()
            own.wait()
            far.wait_recv()
        if p > 0:
            first_step(p - 1)
    first_step(pieces - 1)

    def step(s):
        d = block_of(s)
        for p in range(pieces):
            mine = partial(p, d)
            ring(s - 1, p).wait_recv()
            sent[s, p] = (mine + came[s - 1, p].astype(f32)).astype(bf16)
            ring(s - 1, p).wait_send()
            ring(s, p).start()

    loop(ny - 2, lambda s: step(s + 1))
    for p in range(pieces):
        mine = partial(p, y)
        ring(ny - 2, p).wait_recv()
        out_ref[p * size : (p + 1) * size, :] = (mine + came[ny - 2, p].astype(f32)).astype(bf16)

    for t in range(half):
        for part in range(PARTS):
            for upward in ways(t, part):
                if t > 0 or part >= PARTS // 2:
                    around(t, part, upward).wait_send()
    all_shrinks().wait_send()
    all_weights()[1].wait_send()
    for h in range(2):
        @pl.when(x == 0)
        def _():
            first_hop(h).wait_send()

        if nx == 4:
            @pl.when(x == 1)
            def _():
                second_hop(h, True).wait_send()
                second_hop(h, False).wait_send()

            @pl.when(x == 2)
            def _():
                map_hop(h).wait_send()

    for p in range(pieces):
        normed_copy(p).wait_send()
    for p in range(pieces):
        ring(ny - 2, p).wait_send()


def layer(sizes, *arrays):
    nx, nz, ny = sizes
    tokens = arrays[0].shape[0]
    chunks = tokens // W
    half = nz // 2
    size = tokens // PIECES
    dma = pltpu.SemaphoreType.DMA

    def kernel(*refs):
        layer_kernel(sizes, *refs)

    return pl.pallas_call(
        kernel,
        out_shape=jax.ShapeDtypeStruct((tokens, W), bf16),
        in_specs=[pl.BlockSpec(memory_space=pltpu.MemorySpace.HBM)] * 9,
        out_specs=pl.BlockSpec(memory_space=pltpu.VMEM),
        scratch_shapes=[
            *[pltpu.VMEM(a.shape, a.dtype) for a in arrays[:8]],
            pltpu.VMEM((8 * chunks, W), f32),
            pltpu.VMEM((chunks, W, 8), f32),
            pltpu.VMEM((chunks, 2, W, 2 * W), bf16),
            pltpu.VMEM((chunks, 2, W, 2 * W), bf16),
            pltpu.VMEM((2, 8 + chunks, W), f32),
            pltpu.VMEM((tokens, 2 * W), bf16),
            pltpu.VMEM((tokens, 2 * W), f32),
            pltpu.VMEM((tokens, 2 * W), f32),
            pltpu.VMEM((PARTS, PART_ROWS, 2 * W), bf16),
            pltpu.VMEM((nz, PARTS, PART_ROWS, 2 * W), bf16),
            pltpu.VMEM((nz, 16, W), f32),
            pltpu.VMEM((2, W, W), bf16),
            pltpu.VMEM((2, W, W), bf16),
            pltpu.VMEM((2, W + 16, 2 * W), bf16),
            pltpu.VMEM((2, W + 16, 2 * W), bf16),
            pltpu.VMEM((2, W + 8, 2 * W), f32),
            pltpu.VMEM((ny, 4 * W, W), bf16),
            pltpu.VMEM((2, PIECES, size, 2 * W), bf16),
            pltpu.VMEM((ny - 1, PIECES, size, W), bf16),
            pltpu.VMEM((ny - 1, PIECES, size, W), bf16),
            dma((8,)),
            dma((half, PARTS)), dma((half, PARTS)), dma((half, PARTS)), dma((half, PARTS)),
            dma(()), dma(()),
            dma((8,)), dma((8,)),
            dma(()), dma(()), dma(()),
            dma((PIECES,)), dma((PIECES,)),
            dma((PIECES,)), dma((ny - 1, PIECES)),
        ],
        compiler_params=pltpu.CompilerParams(
            collective_id=0, has_side_effects=True, vmem_limit_bytes=48 << 20
        ),
    )(*[pltpu.with_memory_space_constraint(a, pltpu.MemorySpace.HBM) for a in arrays])


def build(mesh, sizes):
    def local(queries, keys, values, gate, rates, logs, starts, gain, weight):
        return layer(
            sizes, queries, keys, values, gate, rates, logs, starts.reshape(-1, W), gain.reshape(1, W), weight
        )

    both = P("seq", "head")
    placed = (both, both, both, both, P("head", "seq"), P("head", "seq"), P("seq"), P(), P("head", None))
    return jax.shard_map(local, mesh=mesh, in_specs=placed, out_specs=both, check_vma=False)


def solution(mesh):
    return build(mesh, (NX, NZ, NY))
```

```python
import jax
import jax.numpy as jnp
from jax import lax
from jax.experimental import pallas as pl
from jax.experimental.pallas import tpu as pltpu
from jax.sharding import PartitionSpec as P

W = 128
NX, NZ, NY = 4, 8, 8
PIECES = 4
PARTS = 2
PART_ROWS = 2 * W // PARTS
f32, bf16 = jnp.float32, jnp.bfloat16
MESH = pl.DeviceIdType.MESH


def dot(a, b):
    return jnp.dot(a, b, preferred_element_type=f32)


def dot_t(a, b):
    return lax.dot_general(a, b, (((1,), (1,)), ((), ())), preferred_element_type=f32)


def compose(later, earlier):
    g2, y2 = later
    g1, y1 = earlier
    term = jnp.concatenate([g1 * y2[:, :W], y2[:, W:]], axis=1)
    return g1 * g2, g2 * y1 + dot(y2[:, :W].astype(bf16), y1.astype(bf16)) + term


def iotas():
    return lax.broadcasted_iota(jnp.int32, (W, W), 0), lax.broadcasted_iota(jnp.int32, (W, W), 1)


def gather_vectors(k_ref, rate_ref, log_ref, start_ref, rows, cols):
    chunks = k_ref.shape[0] // W
    row, col = iotas()
    eye = row == col
    rows[...] = jnp.zeros_like(rows)
    for c in range(chunks):
        here = slice(c * W, (c + 1) * W)
        rows[8 * c : 8 * c + 2, :] = log_ref[:, here]
        rows[8 * c + 2 : 8 * c + 3, :] = start_ref[c : c + 1, :].astype(f32)
        rows[8 * c + 3 : 8 * c + 5, :] = rate_ref[:, here]
    raw = rows[...]
    upper = (row <= col).astype(f32)
    summed = jnp.dot(raw, upper, precision=lax.Precision.HIGHEST, preferred_element_type=f32)
    kind = lax.broadcasted_iota(jnp.int32, raw.shape, 0) % 8
    vectors = jnp.where(kind < 3, summed, raw)
    rows[...] = vectors
    turned = jnp.transpose(vectors)
    lane = lax.broadcasted_iota(jnp.int32, (W, 8), 1)
    for c in range(chunks):
        here = slice(c * W, (c + 1) * W)
        kf = k_ref[here, :].astype(f32)
        rk_c = lax.rsqrt(jnp.sum(kf * kf, axis=1, keepdims=True) + 1e-6)
        rows[8 * c + 5 : 8 * c + 6, :] = jnp.sum(jnp.where(eye, rk_c, 0.0), axis=0, keepdims=True)
        cols[c] = jnp.where(lane == 5, rk_c, turned[:, 8 * c : 8 * c + 8])


def chunk_at(ref, c):
    return ref[c * W : (c + 1) * W, :] if isinstance(c, int) else ref[pl.ds(pl.multiple_of(c * W, W), W), :]


def vectors_at(rows, cols, c):
    at = slice(8 * c, 8 * c + 8) if isinstance(c, int) else pl.ds(pl.multiple_of(c * 8, 8), 8)
    return rows[at, :], cols[c]


def decay_of(vec_r, vec_c, h):
    row, col = iotas()
    same = (row >= col) & (vec_r[2:3] == vec_c[:, 2:3])
    return jnp.exp(jnp.where(same, vec_c[:, h : h + 1] - vec_r[h : h + 1], -1e9))


def twin(pair):
    zero = jnp.zeros((pair.shape[0], W), pair.dtype)
    return jnp.concatenate(
        [jnp.concatenate([pair[:, :W], zero], axis=1), jnp.concatenate([zero, pair[:, W:]], axis=1)], axis=0
    )


def refine(inverse, coupling, size):
    row, col = pair_iotas()
    block = (row // (4 * size) == col // (4 * size)) & (row // size > col // size)
    inv_b = inverse.astype(bf16)
    n = dot(inv_b, twin(jnp.where(block, coupling, 0.0).astype(bf16))).astype(bf16)
    squared = dot(n, twin(n)).astype(bf16)
    once = inverse - dot(n, twin(inv_b))
    return once + dot(squared, twin(once.astype(bf16)))


def pair_iotas():
    row = lax.broadcasted_iota(jnp.int32, (W, 2 * W), 0)
    col = lax.broadcasted_iota(jnp.int32, (W, 2 * W), 1)
    return row, lax.rem(col, W)


def chunk_maps(chunks, k_ref, v_ref, rows, cols, both_ref):
    row, col = pair_iotas()

    def side(parts):
        return jnp.concatenate(parts, axis=1)

    found = []
    for c in range(chunks):
        vec_r, vec_c = vectors_at(rows, cols, c)
        kc = chunk_at(k_ref, c)
        kk = dot_t(kc, kc) * vec_c[:, 5:6] * vec_r[5:6]
        coupling = side([vec_c[:, 3 + h : 4 + h] * kk * decay_of(vec_r, vec_c, h) for h in range(2)])
        near = jnp.where((row // 2 == col // 2) & (row >= col), -coupling, 0.0)
        found.append([coupling, jnp.where(row == col, 1.0, near)])
    for size in (2, 8, 32):
        for entry in found:
            entry[1] = refine(entry[1], entry[0], size)
    moves = {}
    for c in range(chunks):
        vec_r, vec_c = vectors_at(rows, cols, c)
        kc = chunk_at(k_ref, c)
        k_turned = jnp.transpose(kc.astype(f32)).astype(bf16)
        inverse = found[c][1]
        rk_r = vec_r[5:6]
        reset_r, reset_c = vec_r[2:3], vec_c[:, 2:3]
        reset_last = reset_r[:, W - 1 : W]
        rates = [vec_r[3 + h : 4 + h] for h in range(2)]
        heads = [jnp.where(reset_r == 0.0, jnp.exp(vec_r[h : h + 1]), 0.0) for h in range(2)]
        scale = side([rates[h] * heads[h] * rk_r for h in range(2)])
        erase = dot((inverse * scale).astype(bf16), twin(side([kc, kc])))
        write = dot((inverse * side(rates)).astype(bf16), twin(chunk_at(v_ref, c)))
        for h in range(2):
            lanes = slice(h * W, (h + 1) * W)
            g_c = vec_c[:, h : h + 1]
            g_last = vec_r[h : h + 1, W - 1 : W]
            tail_c = jnp.where(reset_c == reset_last, jnp.exp(g_last - g_c), 0.0)
            whole = jnp.where(reset_last == 0.0, jnp.exp(g_last), 0.0)
            both = side([erase[:, lanes], write[:, lanes]])
            both_ref[c, h] = both.astype(bf16)
            moved = dot(k_turned, (both * (tail_c * vec_c[:, 5:6])).astype(bf16))
            moves[c, h] = (whole, side([-moved[:, :W], moved[:, W:]]))
    return moves


def prefix_map(levels, count):
    found = None
    for depth in reversed(range(len(levels))):
        if count >> depth & 1:
            here = levels[depth][(count >> depth) - 1]
            found = here if found is None else compose(here, found)
    return found


def token_outputs(
    first, count, q_ref, k_ref, rows, cols, both_ref, maps_ref, gam_ref, qeff_ref, att_ref,
    gate_ref, gain_ref, open_ref,
):
    scores = []
    for c in range(first, first + count):
        vec_r, vec_c = vectors_at(rows, cols, c)
        qc = chunk_at(q_ref, c)
        qf = qc.astype(f32)
        rq_c = lax.rsqrt(jnp.sum(qf * qf, axis=1, keepdims=True) + 1e-6)
        qk = dot_t(qc, chunk_at(k_ref, c)) * rq_c * vec_r[5:6]
        scores.append((qf * rq_c, [(qk * decay_of(vec_r, vec_c, h)).astype(bf16) for h in range(2)]))
    scored = [
        [dot(scores[c - first][1][h], both_ref[c, h]) for h in range(2)] for c in range(first, first + count)
    ]
    for c in range(first, first + count):
        here = slice(c * W, (c + 1) * W)
        vec_r, vec_c = vectors_at(rows, cols, c)
        for h in range(2):
            g_c, reset_c = vec_c[:, h : h + 1], vec_c[:, 2:3]
            head_c = jnp.where(reset_c == 0.0, jnp.exp(g_c), 0.0)
            mine = scored[c - first][h]
            reach = scores[c - first][0] * head_c - mine[:, :W]
            product = dot(reach.astype(bf16), maps_ref[c, h])
            lanes = slice(h * W, (h + 1) * W)
            gam = gam_ref[h, 8 + c : 9 + c, :]
            qeff_ref[here, lanes] = (product[:, :W] + gam * reach).astype(bf16)
            att_ref[here, lanes] = product[:, W:] + mine[:, W:]
            gate = gate_ref[here, lanes].astype(f32)
            open_ref[here, lanes] = gain_ref[...] * (gate / (1.0 + jnp.exp(-gate)))


def layer_kernel(
    sizes, q_hbm, k_hbm, v_hbm, gate_hbm, rate_hbm, log_hbm, start_hbm, gain_hbm, w_ref, out_ref,
    q_ref, k_ref, v_ref, gate_ref, rate_ref, log_ref, start_ref, gain_ref,
    rows, cols, both_ref, maps_ref, gam_ref, qeff_ref, att_ref, open_ref,
    msg, got, shrinks, hop_out, hop_in, map_out, map_in, lead, weights, normed, sent, came,
    load, right_s, right_r, left_s, left_r, shrink_s, shrink_r, hop_s, hop_r,
    w_own, w_s, w_r, n_s, n_r, ring_s, ring_r,
):
    nx, nz, ny = sizes
    chunks = q_ref.shape[0] // W
    seq, head = lax.axis_index("seq"), lax.axis_index("head")
    x, z = seq // nz, lax.rem(seq, nz)
    y, core = head // 2, lax.rem(head, 2)
    half = nz // 2
    step_y = 1 - 2 * core

    def seq_of(x_at, z_at):
        return lax.rem(x_at + nx, nx) * nz + lax.rem(z_at + nz, nz)

    def head_of(y_at, core_at):
        return lax.rem(y_at + ny, ny) * 2 + core_at

    next_row, last_row = (seq_of(x + 1, z), head), (seq_of(x - 1, z), head)
    third_row = (seq_of(x + 2, z), head)
    sibling = (seq, head_of(y, 1 - core))
    ahead, behind = (seq, head_of(y + 1, core)), (seq, head_of(y - 1, core))
    target = (seq, head_of(y + step_y, core))
    column = [(seq_of(x, z + dz), head) for dz in range(nz)]
    above, below = column[1], column[nz - 1]

    barrier = pltpu.get_barrier_semaphore()
    greeted = (*column[1:], next_row, last_row, third_row, sibling, ahead, behind)
    for other in greeted:
        pl.semaphore_signal(barrier, inc=1, device_id=other, device_id_type=MESH)

    pairs = (
        (k_hbm, k_ref), (log_hbm, log_ref), (rate_hbm, rate_ref), (start_hbm, start_ref), (q_hbm, q_ref),
        (v_hbm, v_ref), (gate_hbm, gate_ref), (gain_hbm, gain_ref),
    )
    loads = [pltpu.make_async_copy(src, dst, load.at[n]) for n, (src, dst) in enumerate(pairs)]
    for copy in loads:
        copy.start()

    def remote(src, dst, send, recv, device):
        return pltpu.make_async_remote_copy(
            src_ref=src, dst_ref=dst, send_sem=send, recv_sem=recv, device_id=device, device_id_type=MESH
        )

    def around(t, h, upward):
        owner = lax.rem(z - t + nz, nz) if upward else lax.rem(z + t, nz)
        src = msg.at[h] if t == 0 else got.at[owner, h]
        if upward:
            return remote(src, got.at[owner, h], right_s.at[t, h], right_r.at[t, h], above)
        return remote(src, got.at[owner, h], left_s.at[t, h], left_r.at[t, h], below)

    def ways(t, h):
        return (True, False) if t < half - 1 else ((True,) if h < PARTS // 2 else (False,))

    def shrink_copy(dz):
        return remote(shrinks.at[z], shrinks.at[z], shrink_s, shrink_r, column[dz])

    def all_shrinks():
        return remote(shrinks.at[: nz - 1], shrinks.at[: nz - 1], shrink_s, shrink_r, column[1])

    def weight_copies(d):
        mine = pl.ds(pl.multiple_of((2 * d + core) * W, W), W)
        theirs = pl.ds(pl.multiple_of((2 * d + 1 - core) * W, W), W)
        own = pltpu.make_async_copy(w_ref.at[:, mine], weights.at[d, : 2 * W], w_own)
        far = remote(w_ref.at[:, theirs], weights.at[d, 2 * W :], w_s, w_r, sibling)
        return own, far

    def all_weights():
        near, rest = weights.at[:, : 2 * W], weights.at[:, 2 * W :]
        return pltpu.make_async_copy(near, near, w_own), remote(rest, rest, w_s, w_r, sibling)

    for n in range(4):
        loads[n].wait()
    gather_vectors(k_ref, rate_ref, log_ref, start_ref, rows, cols)
    loads[5].wait()

    def outputs(first, count):
        token_outputs(
            first, count, q_ref, k_ref, rows, cols, both_ref, maps_ref, gam_ref, qeff_ref, att_ref,
            gate_ref, gain_ref, open_ref,
        )

    def pass_on(t, h):
        for upward in (True, False):
            around(t - 1, h, upward).wait_recv()
            if upward in ways(t, h):
                around(t, h, upward).start()

    def loop(count, body):
        def wrapped(i, carry):
            body(i)
            return carry

        lax.fori_loop(0, count, wrapped, 0)

    moves = chunk_maps(chunks, k_ref, v_ref, rows, cols, both_ref)
    trees = []
    for h in range(2):
        tree = [[moves[c, h] for c in range(chunks)]]
        while len(tree[-1]) > 1:
            last = tree[-1]
            tree.append([compose(last[n + 1], last[n]) for n in range(0, len(last), 2)])
        trees.append(tree)
        gam_ref[h, 0:8, :] = jnp.broadcast_to(tree[-1][0][0], (8, W))
    pl.semaphore_wait(barrier, len(greeted))
    def send_own(h):
        for n in range(PARTS // 2):
            part = h * PARTS // 2 + n
            msg[part] = trees[h][-1][0][1][n * PART_ROWS : (n + 1) * PART_ROWS].astype(bf16)
            for upward in (True, False):
                around(0, part, upward).start()

    send_own(0)
    shrinks[z] = jnp.concatenate([gam_ref[0, 0:8, :], gam_ref[1, 0:8, :]], axis=0)
    for dz in range(1, nz):
        shrink_copy(dz).start()
    for d in range(ny):
        own, far = weight_copies(d)
        own.start()
        far.start()
    shares = [chunks * n // half for n in range(half + 1)]
    for n in (4, 6, 7):
        loads[n].wait()
    for h in range(2):
        maps_ref[0, h] = jnp.zeros((W, 2 * W), bf16)
        gam_ref[h, 8:9, :] = jnp.ones((1, W), f32)

    def prefixes(first, count):
        for c in range(max(first, 1), first + count):
            for h in range(2):
                gam, mat = prefix_map(trees[h], c)
                maps_ref[c, h] = mat.astype(bf16)
                gam_ref[h, 8 + c : 9 + c, :] = jnp.broadcast_to(gam, (1, W))

    prefixes(0, shares[1])
    outputs(0, shares[1])
    for part in range(PARTS // 2):
        for upward in ways(0, part):
            around(0, part, upward).wait_send()
    send_own(1)
    got[z] = msg[...]

    for t in range(1, half):
        for part in range(PARTS):
            pass_on(t, part)
            if part == PARTS // 2 - 1:
                prefixes(shares[t], shares[t + 1] - shares[t])
                outputs(shares[t], shares[t + 1] - shares[t])
    for part in range(PARTS):
        for upward in ways(half - 1, part):
            around(half - 1, part, upward).wait_recv()
    all_shrinks().wait_recv()

    def single(at, h):
        pair = [got[at, n] for n in range(h * PARTS // 2, (h + 1) * PARTS // 2)]
        return shrinks[at, 8 * h : 8 * h + 1, 0:1], jnp.concatenate(pair, axis=0).astype(f32)

    zero = jnp.zeros((W, 2 * W), f32)
    whole_row, prefix = [], []
    for h in range(2):
        level = [single(at, h) for at in range(nz)]
        levels = []
        while len(level) > 1:
            levels.append(level)
            level = [compose(level[n + 1], level[n]) for n in range(0, len(level), 2)]
        whole_row.append(level[0])
        ahead_map = None
        for depth in reversed(range(len(levels))):
            here = levels[depth]
            count = lax.shift_right_logical(z, depth)
            gam, mat = jnp.ones((1, 1), f32), zero
            for n in range(0, len(here), 2):
                take = count == n + 1
                gam = jnp.where(take, here[n][0], gam)
                mat = jnp.where(take, here[n][1], mat)
            ahead_map = (gam, mat) if ahead_map is None else compose((gam, mat), ahead_map)
        prefix.append(ahead_map)

    def enter(state, came_in):
        gam, mat = state
        return gam * came_in.astype(f32) + dot(mat[:, :W].astype(bf16), came_in) + mat[:, W:]

    def first_hop(h):
        return remote(hop_out.at[h], hop_in.at[h], hop_s.at[h], hop_r.at[h], next_row)

    def map_hop(h):
        return remote(map_out.at[h], map_in.at[h], hop_s.at[2 + h], hop_r.at[2 + h], next_row)

    def second_hop(h, far):
        n = 4 + 2 * far + h
        return remote(hop_out.at[h], hop_in.at[h], hop_s.at[n], hop_r.at[n], third_row if far else next_row)

    if nx not in (2, 4):
        raise ValueError("rows")

    @pl.when(x == 0)
    def _():
        hop_in[...] = jnp.zeros_like(hop_in)
        for h in range(2):
            hop_out[h] = whole_row[h][1][:, W:].astype(bf16)
            first_hop(h).start()

    @pl.when(x == 1)
    def _():
        for h in range(2):
            first_hop(h).wait_recv()
            if nx == 4:
                hop_out[h] = enter(whole_row[h], hop_in[h]).astype(bf16)
                second_hop(h, True).start()
                second_hop(h, False).start()

    if nx == 4:
        @pl.when(x == 2)
        def _():
            for h in range(2):
                gam, mat = whole_row[h]
                map_out[h, :W] = mat.astype(bf16)
                hi = gam.astype(bf16).astype(f32)
                mid = (gam - hi).astype(bf16).astype(f32)
                low = gam - hi - mid
                at = lax.broadcasted_iota(jnp.int32, (16, 2 * W), 0)
                map_out[h, W:] = jnp.where(
                    at == 0, hi, jnp.where(at == 1, mid, jnp.where(at == 2, low, 0.0))
                ).astype(bf16)
                map_hop(h).start()

        @pl.when(x == 3)
        def _():
            for h in range(2):
                map_hop(h).wait_recv()
                gam = jnp.sum(map_in[h, W:].astype(f32), axis=0, keepdims=True)[:, 0:1]
                gam, mat = compose(prefix[h], (gam, map_in[h, :W].astype(f32)))
                lead[h, :W] = mat
                lead[h, W:] = jnp.broadcast_to(gam, (8, 2 * W))
            for h in range(2):
                second_hop(h, True).wait_recv()

        @pl.when(x == 2)
        def _():
            for h in range(2):
                second_hop(h, False).wait_recv()

    @pl.when(x < 3)
    def _():
        for h in range(2):
            lead[h, :W] = prefix[h][1]
            lead[h, W:] = jnp.broadcast_to(prefix[h][0], (8, 2 * W))

    entering = [
        enter((lead[h, W : W + 1, 0:1], lead[h, :W]), hop_in[h]).astype(bf16) for h in range(2)
    ]

    pieces = PIECES
    size = qeff_ref.shape[0] // pieces

    def normed_copy(p):
        return remote(normed.at[0, p], normed.at[1, p], n_s.at[p], n_r.at[p], sibling)

    def make_normed(p):
        here = slice(p * size, (p + 1) * size)
        for h in range(2):
            lanes = slice(h * W, (h + 1) * W)
            attended = att_ref[here, lanes] + dot(qeff_ref[here, lanes], entering[h])
            scale = lax.rsqrt(jnp.mean(attended * attended, axis=1, keepdims=True) + 1e-6)
            normed[0, p, :, lanes] = (attended * scale * open_ref[here, lanes]).astype(bf16)

    def partial(p, d):
        return dot(normed[0, p], weights[d, : 2 * W]) + dot(normed[1, p], weights[d, 2 * W :])

    def ring(s, p):
        return remote(sent.at[s, p], came.at[s, p], ring_s.at[p], ring_r.at[s, p], target)

    def block_of(s):
        return lax.rem(y - step_y * (s + 1) + 2 * ny, ny)

    def first_step(p):
        normed_copy(p).wait_recv()
        sent[0, p] = partial(p, block_of(0)).astype(bf16)
        ring(0, p).start()

    for p in range(pieces):
        make_normed(p)
        normed_copy(p).start()
        if p == 0:
            own, far = all_weights()
            own.wait()
            far.wait_recv()
        if p > 0:
            first_step(p - 1)
    first_step(pieces - 1)

    def step(s):
        d = block_of(s)
        for p in range(pieces):
            mine = partial(p, d)
            ring(s - 1, p).wait_recv()
            sent[s, p] = (mine + came[s - 1, p].astype(f32)).astype(bf16)
            ring(s - 1, p).wait_send()
            ring(s, p).start()

    loop(ny - 2, lambda s: step(s + 1))
    for p in range(pieces):
        mine = partial(p, y)
        ring(ny - 2, p).wait_recv()
        out_ref[p * size : (p + 1) * size, :] = (mine + came[ny - 2, p].astype(f32)).astype(bf16)

    for t in range(half):
        for part in range(PARTS):
            for upward in ways(t, part):
                if t > 0 or part >= PARTS // 2:
                    around(t, part, upward).wait_send()
    all_shrinks().wait_send()
    all_weights()[1].wait_send()
    for h in range(2):
        @pl.when(x == 0)
        def _():
            first_hop(h).wait_send()

        if nx == 4:
            @pl.when(x == 1)
            def _():
                second_hop(h, True).wait_send()
                second_hop(h, False).wait_send()

            @pl.when(x == 2)
            def _():
                map_hop(h).wait_send()

    for p in range(pieces):
        normed_copy(p).wait_send()
    for p in range(pieces):
        ring(ny - 2, p).wait_send()


def layer(sizes, *arrays):
    nx, nz, ny = sizes
    tokens = arrays[0].shape[0]
    chunks = tokens // W
    half = nz // 2
    size = tokens // PIECES
    dma = pltpu.SemaphoreType.DMA

    def kernel(*refs):
        layer_kernel(sizes, *refs)

    return pl.pallas_call(
        kernel,
        out_shape=jax.ShapeDtypeStruct((tokens, W), bf16),
        in_specs=[pl.BlockSpec(memory_space=pltpu.MemorySpace.HBM)] * 9,
        out_specs=pl.BlockSpec(memory_space=pltpu.VMEM),
        scratch_shapes=[
            *[pltpu.VMEM(a.shape, a.dtype) for a in arrays[:8]],
            pltpu.VMEM((8 * chunks, W), f32),
            pltpu.VMEM((chunks, W, 8), f32),
            pltpu.VMEM((chunks, 2, W, 2 * W), bf16),
            pltpu.VMEM((chunks, 2, W, 2 * W), bf16),
            pltpu.VMEM((2, 8 + chunks, W), f32),
            pltpu.VMEM((tokens, 2 * W), bf16),
            pltpu.VMEM((tokens, 2 * W), f32),
            pltpu.VMEM((tokens, 2 * W), f32),
            pltpu.VMEM((PARTS, PART_ROWS, 2 * W), bf16),
            pltpu.VMEM((nz, PARTS, PART_ROWS, 2 * W), bf16),
            pltpu.VMEM((nz, 16, W), f32),
            pltpu.VMEM((2, W, W), bf16),
            pltpu.VMEM((2, W, W), bf16),
            pltpu.VMEM((2, W + 16, 2 * W), bf16),
            pltpu.VMEM((2, W + 16, 2 * W), bf16),
            pltpu.VMEM((2, W + 8, 2 * W), f32),
            pltpu.VMEM((ny, 4 * W, W), bf16),
            pltpu.VMEM((2, PIECES, size, 2 * W), bf16),
            pltpu.VMEM((ny - 1, PIECES, size, W), bf16),
            pltpu.VMEM((ny - 1, PIECES, size, W), bf16),
            dma((8,)),
            dma((half, PARTS)), dma((half, PARTS)), dma((half, PARTS)), dma((half, PARTS)),
            dma(()), dma(()),
            dma((8,)), dma((8,)),
            dma(()), dma(()), dma(()),
            dma((PIECES,)), dma((PIECES,)),
            dma((PIECES,)), dma((ny - 1, PIECES)),
        ],
        compiler_params=pltpu.CompilerParams(
            collective_id=0, has_side_effects=True, vmem_limit_bytes=48 << 20
        ),
    )(*[pltpu.with_memory_space_constraint(a, pltpu.MemorySpace.HBM) for a in arrays])


def build(mesh, sizes):
    def local(queries, keys, values, gate, rates, logs, starts, gain, weight):
        return layer(
            sizes, queries, keys, values, gate, rates, logs, starts.reshape(-1, W), gain.reshape(1, W), weight
        )

    both = P("seq", "head")
    placed = (both, both, both, both, P("head", "seq"), P("head", "seq"), P("seq"), P(), P("head", None))
    return jax.shard_map(local, mesh=mesh, in_specs=placed, out_specs=both, check_vma=False)


def solution(mesh):
    return build(mesh, (NX, NZ, NY))
```
